32 devices in a mesh: groups: 2 (over y), docs: 8 (over z, x), help: 2 (over core).
Axes of the slice: x: 2, y: 2, z: 4, core: 2. Of those that a mesh axis runs over, the one named last changes fastest.
Arguments:
- token_states: bfloat16 [4096, 2, 1024], P(('groups', 'docs', 'help')), parts along dimension 0, may hold values from -6 to 6
- lengths: int32 [4096], P(('groups', 'docs', 'help')), parts along dimension 0, may hold values from 1 to 2
- cluster_id: int32 [4096], P(('groups', 'docs', 'help')), parts along dimension 0, may hold values from 0 to 7, as said below
- proj_weight: bfloat16 [1024, 1024], replicated, may hold values from -0.1875 to 0.1875
- proj_bias: float32 [1024], replicated, may hold values from -4 to 4
Outputs:
- max_sim: float32 [4096], P(('groups', 'docs', 'help')), parts along dimension 0
The draws below stay inside these ranges and needn't reach their ends.
There are 2 independent parts, one for each index of `groups`. The reference program is written for one: setup_inputs(seed, part) draws one part's arguments, and reference() takes and returns one part's arrays. A program takes and returns all parts, laid end to end along the dimension named above; an argument that names none is the same for every part. Nothing has to cross between parts.
Inputs may be any that keep to these rules, and one draw needn't show every extreme that they name: `cluster_id`: clusters 1 * k to 1 * k + 1 - 1 form owner k. Among the 128 documents of one device (aligned blocks of the document dimension), at most 32 belong to one owner, and in every draw one owner gets exactly 32 documents from every device.
All inputs are finite; a program needn't handle non-finite values.
Results may differ from the reference program's by a relative error of at most 0.0003.
Values may be sent and summed in bfloat16 or wider, within the bound.
A program may use at most 64 MiB of HBM per device.

```python
import jax
import jax.numpy as jnp
from jax import lax

D = 1024
SEQ = 2
DOC_DEV = 128
CL_OWN = 1
CAP = 32
DOCS = 2048
CLUSTERS = 8


def draw_cluster_id(key, part):
    blocks = DOCS // DOC_DEV
    owners = CLUSTERS // CL_OWN
    position_count = owners * CAP
    key_hot, key_pop, key_score, key_order, key_local = jax.random.split(key, 5)
    busiest_holder = jax.random.randint(key_hot, (), 0, owners)
    frequent_clusters = jax.random.randint(key_pop, (owners,), 0, 4)
    position_holder = jnp.arange(position_count, dtype=jnp.int32) // CAP
    extra_reward = frequent_clusters[position_holder] + jnp.where(position_holder == busiest_holder, 8, 0)
    random_jitter = jax.random.randint(key_score, (blocks, position_count), 0, 65536)
    duplicate_scores = (extra_reward[None, :] * 16384 + random_jitter) * position_count + jnp.arange(position_count, dtype=jnp.int32)[None, :]
    top_vals, chosen = lax.top_k(duplicate_scores, DOC_DEV)
    owner_rows = chosen // CAP
    shuffle_keys = jax.random.randint(key_order, (blocks, DOC_DEV), 0, 65536) * DOC_DEV + jnp.arange(DOC_DEV, dtype=jnp.int32)[None, :]
    shuffled_order = jnp.argsort(shuffle_keys, axis=1)
    owner_rows = jnp.take_along_axis(owner_rows, shuffled_order, axis=1).reshape(DOCS)
    local_idx = jax.random.randint(key_local, (DOCS,), 0, CL_OWN)
    return (owner_rows * CL_OWN + local_idx).astype(jnp.int32)


def with_ends(array, stream_key, least, top_value):
    longest = array.shape.index(max(array.shape))
    spots = []
    for shift in (0, 1):
        where = [jax.random.randint(jax.random.fold_in(stream_key, axis), (), 0, length) for axis, length in enumerate(array.shape)]
        where[longest] = (where[longest] + shift) % array.shape[longest]
        spots.append(tuple(where))
    return array.at[spots[0]].set(least).at[spots[1]].set(top_value)


def block_scale(rng, dims, cuts, low, largest):
    gain = 1.0
    for axis_at, blocks in cuts:
        heights = jax.random.uniform(jax.random.fold_in(jax.random.fold_in(rng, 6), axis_at), (blocks,), jnp.float32, low / len(cuts), largest / len(cuts))
        gain = gain * jnp.repeat(jnp.exp(heights), dims[axis_at] // blocks).reshape((-1,) + (1,) * (len(dims) - 1 - axis_at))
    return gain


def centred(own_key, dims, width, most, cuts=(), kind=jnp.bfloat16):
    entries = width * jax.random.normal(own_key, dims, jnp.float32)
    if cuts:
        entries = entries * block_scale(own_key, dims, cuts, -0.22, 0.18)
    return jnp.clip(entries, -most, most).astype(kind)


def setup_inputs(seed: int = 0, part: int = 0) -> dict:
    arg_keys = jax.random.split(jax.random.key(seed), 6)
    part_splits = jax.random.split(jax.random.fold_in(arg_keys[5], part), 6)
    return {
        "token_states": centred(part_splits[0], (DOCS, SEQ, D), 1.0, 6.0, ((0, 16),)),
        "lengths": with_ends(jax.random.randint(part_splits[1], (DOCS,), 1, SEQ + 1), jax.random.fold_in(part_splits[1], 1), 1, SEQ).astype(jnp.int32),
        "cluster_id": draw_cluster_id(jax.random.fold_in(jax.random.fold_in(arg_keys[5], part), 71), part),
        "proj_weight": centred(arg_keys[3], (D, D), D ** -0.5, 0.1875),
        "proj_bias": centred(arg_keys[4], (D,), 1.0, 4.0, (), jnp.float32),
    }


def embed_docs(token_states, lengths, proj_weight, proj_bias):
    seq_len = token_states.shape[1]
    feat_dim = token_states.shape[2]

    def embed_block(pieces):
        states, counts = pieces
        token_mask = (jnp.arange(seq_len, dtype=jnp.int32)[None, :] < counts[:, None]).astype(jnp.float32)
        summed = jnp.einsum('rsd,rs->rd', states.astype(jnp.float32), token_mask)
        pooled = (summed / counts[:, None].astype(jnp.float32)).astype(jnp.bfloat16)
        hidden = jnp.tanh(jnp.dot(pooled, proj_weight, preferred_element_type=jnp.float32) + proj_bias)
        factor = lax.rsqrt(lax.optimization_barrier(jnp.sum(hidden * hidden, axis=1, keepdims=True)) + 1e-06)
        return (hidden * factor).astype(jnp.bfloat16)
    block_count = token_states.shape[0] // DOC_DEV
    shaped = token_states.reshape(block_count, DOC_DEV, seq_len, feat_dim)
    counts = lengths.reshape(block_count, DOC_DEV)
    return lax.map(embed_block, (shaped, counts)).reshape(token_states.shape[0], feat_dim)

def reference(token_states, lengths, cluster_id, proj_weight, proj_bias):
    embedded = embed_docs(token_states, lengths, proj_weight, proj_bias)
    total = cluster_id.shape[0]
    feat_dim = embedded.shape[1]
    sort_order = jnp.argsort(cluster_id, stable=True).astype(jnp.int32)
    sorted_ids = cluster_id[sort_order]
    sorted_emb = embedded[sort_order]
    reach = 4 * DOC_DEV
    row_block = min(512, total)
    span = row_block + 2 * reach
    edge_ids = jnp.full((reach,), -2, jnp.int32)
    edge_emb = jnp.zeros((reach, feat_dim), embedded.dtype)
    pad_ids = jnp.concatenate([edge_ids, sorted_ids, edge_ids])
    pad_emb = jnp.concatenate([edge_emb, sorted_emb, edge_emb], axis=0)

    def block_max(start):
        row_emb = lax.dynamic_slice_in_dim(sorted_emb, start, row_block, 0)
        row_ids = lax.dynamic_slice_in_dim(sorted_ids, start, row_block, 0)
        col_emb = lax.dynamic_slice_in_dim(pad_emb, start, span, 0)
        col_ids = lax.dynamic_slice_in_dim(pad_ids, start, span, 0)
        duplicate_scores = jnp.einsum('rd,cd->rc', row_emb.astype(jnp.float32), col_emb.astype(jnp.float32))
        row_pos = start + jnp.arange(row_block, dtype=jnp.int32)
        col_pos = start - reach + jnp.arange(span, dtype=jnp.int32)
        match = (row_ids[:, None] == col_ids[None, :]) & (row_pos[:, None] != col_pos[None, :])
        return lax.optimization_barrier(jnp.max(jnp.where(match, duplicate_scores, -1.0), axis=1))
    starts = jnp.arange(total // row_block, dtype=jnp.int32) * row_block
    sorted_max = lax.map(block_max, starts).reshape(total)
    return jnp.zeros((total,), jnp.float32).at[sort_order].set(sorted_max)
```

```python
import jax
import jax.numpy as jnp
from jax import lax
from jax.experimental import pallas as pl
from jax.experimental.pallas import tpu as pltpu
from jax.sharding import PartitionSpec as P

CL_OWN = 1


def partner(value, axis, bit):
    return lax.ppermute(value, axis, [(i, i ^ 1 << bit) for i in range(lax.axis_size(axis))])


def slot_maxima(own_emb, own_ids, self_pos, col_emb, col_ids):
    row_total = own_emb.shape[0]
    block = min(row_total, 512)
    col_pos = lax.broadcasted_iota(jnp.int32, (col_emb.shape[0],), 0)

    def block_max(pieces):
        part_emb, part_ids, part_self = pieces
        duplicate_scores = jnp.einsum(
            "rd,cd->rc", part_emb, col_emb, preferred_element_type=jnp.float32
        )
        match = (
            (part_ids[:, None] == col_ids[None, :])
            & (col_ids[None, :] >= 0)
            & (part_self[:, None] != col_pos[None, :])
        )
        return jnp.max(jnp.where(match, duplicate_scores, -1.0), axis=1)

    steps_count = row_total // block
    result = lax.map(
        block_max,
        (
            own_emb.reshape(steps_count, block, own_emb.shape[1]),
            own_ids.reshape(steps_count, block),
            self_pos.reshape(steps_count, block),
        ),
    )
    return result.reshape(row_total)


def body(token_states, lengths, cluster_id, proj_weight, proj_bias):
    row_count, seq_len, feat_dim = token_states.shape
    owners = lax.axis_size("docs")
    slot_cap = 2 * row_count // owners
    position_count = owners * slot_cap
    token_mask = (
        lax.broadcasted_iota(jnp.int32, (row_count, seq_len), 1) < lengths[:, None]
    ).astype(jnp.bfloat16)
    summed = jnp.einsum("rsd,rs->rd", token_states, token_mask, preferred_element_type=jnp.float32)
    pooled = (summed / lengths[:, None].astype(jnp.float32)).astype(jnp.bfloat16)
    hidden = jnp.tanh(jnp.dot(pooled, proj_weight, preferred_element_type=jnp.float32) + proj_bias)
    factor = lax.rsqrt(jnp.sum(hidden * hidden, axis=1, keepdims=True) + 1e-06)
    embedded = (hidden * factor).astype(jnp.bfloat16)
    dest_owner = cluster_id // CL_OWN
    same_owner = dest_owner[:, None] == dest_owner[None, :]
    earlier = lax.broadcasted_iota(jnp.int32, (row_count, row_count), 1) < lax.broadcasted_iota(
        jnp.int32, (row_count, row_count), 0
    )
    slot_rank = jnp.sum((same_owner & earlier).astype(jnp.int32), axis=1)
    target = dest_owner * slot_cap + slot_rank
    chooser = lax.broadcasted_iota(jnp.int32, (position_count, row_count), 0) == target[None, :]
    packed = jnp.dot(
        chooser.astype(jnp.bfloat16), embedded, preferred_element_type=jnp.float32
    ).astype(jnp.bfloat16)
    packed_ids = jnp.max(jnp.where(chooser, cluster_id[None, :], -1), axis=1)
    own_emb, own_ids = (
        lax.all_to_all(packed, "docs", split_axis=0, concat_axis=0, tiled=True),
        lax.all_to_all(packed_ids, "docs", split_axis=0, concat_axis=0, tiled=True),
    )
    mate_emb, mate_ids = partner((own_emb, own_ids), "help", 0)
    col_emb = jnp.concatenate([own_emb, mate_emb], axis=0)
    col_ids = jnp.concatenate([own_ids, mate_ids], axis=0)
    self_pos = lax.broadcasted_iota(jnp.int32, (position_count,), 0)
    maxima = slot_maxima(own_emb, own_ids, self_pos, col_emb, col_ids)
    returned = lax.all_to_all(maxima, "docs", split_axis=0, concat_axis=0, tiled=True)
    return jnp.max(jnp.where(chooser, returned[:, None], -3.0), axis=0)


ROWS = 4
CORES = 2
CHUNKS = 4
SAME = 4.0
SIBLING, CORNER, NEAR_TOO, END_TOO, AFTER = range(5)
ACROSS, OUTER, NEAR, END = (AFTER + 1 + CHUNKS * at for at in range(4))
FLOWS = END + CHUNKS


def meet_kernel(
    states_hbm,
    lengths_hbm,
    ids_hbm,
    weight_hbm,
    bias_hbm,
    out_ref,
    lengths_ref,
    bias_ref,
    states_ref,
    weight_ref,
    ids_ref,
    blocks_ref,
    marks_ref,
    detour_ref,
    best_ref,
    folded_ref,
    given_ref,
    taken_ref,
    small_sem,
    states_sem,
    weight_sem,
    block_send,
    block_recv,
    detour_recv,
    ids_send,
    ids_recv,
    best_send,
    best_recv,
):
    row_count, seq_len, feat_dim = states_ref.shape
    lines = blocks_ref.shape[0]
    columns = lines // CORES
    chunk = row_count // CHUNKS
    hub = ROWS - 2
    group = lax.axis_index("groups")
    docs = lax.axis_index("docs")
    core = lax.axis_index("help")
    depth = docs // columns
    col = docs % columns
    row = depth + group * (ROWS - 1 - 2 * depth)
    far_col = columns - 1 - col
    far_core = CORES - 1 - core
    line = col * CORES + core
    sibling_line = col * CORES + far_core
    across_line = far_col * CORES + core

    def device(at_row, at_col, at_core):
        at_depth = at_row + group * (ROWS - 1 - 2 * at_row)
        return {"docs": at_depth * columns + at_col, "help": at_core}

    def other_plane(at_row):
        at_depth = at_row + group * (ROWS - 1 - 2 * at_row)
        return {"groups": 1 - group, "docs": at_depth * columns + col, "help": core}

    def spot(at_line, at_row):
        return at_line * ROWS + at_row

    me = spot(line, row)
    sibling_device = device(row, col, far_core)

    small_copies = [
        pltpu.make_async_copy(source, held, small_sem.at[position])
        for position, (source, held) in enumerate(
            [(lengths_hbm, lengths_ref), (ids_hbm, ids_ref.at[me]), (bias_hbm, bias_ref)]
        )
    ]
    for copy in small_copies:
        copy.start()
    states_copy = pltpu.make_async_copy(states_hbm, states_ref, states_sem)
    states_copy.start()
    weight_copy = pltpu.make_async_copy(weight_hbm, weight_ref, weight_sem)
    weight_copy.start()

    barrier = pltpu.get_barrier_semaphore()

    def greet(*wheres):
        for where in wheres:
            pl.semaphore_signal(
                barrier, inc=1, device_id=where, device_id_type=pl.DeviceIdType.MESH
            )

    around = (core == 1) & ((row == 1) | (row == hub))

    def each_to(act):
        @pl.when(row < hub)
        def _():
            for at_core in range(CORES):
                act(device(hub, col, at_core))

        @pl.when(row == 1)
        def _():
            act(device(0, far_col, core))

        @pl.when(row > hub)
        def _():
            act(device(hub, col, core))
            act(device(hub, far_col, core))

        act(device(row, far_col, core))
        act(sibling_device)

    each_to(lambda where: greet(where))

    @pl.when(row == 0)
    def _():
        greet(device(1, col, core), device(1, far_col, core))

    @pl.when(row == 1)
    def _():
        greet(device(0, col, core))

    @pl.when(row == hub)
    def _():
        for at_row in range(hub):
            for at_core in range(CORES):
                greet(device(at_row, col, at_core))
        greet(device(hub + 1, col, core), device(hub + 1, far_col, core))

    @pl.when(around)
    def _():
        greet(other_plane(row))

        @pl.when(row == hub)
        def _():
            greet(other_plane(hub - 1))

    greetings = (
        2
        + 4 * (row < hub)
        + 6 * (row == hub)
        + 2 * (row > hub)
        + around * (1 + (row == hub))
    )

    def send(flow, part, at_line, at_row, where, lane=0):
        rows = blocks_ref.at[at_line, at_row, pl.ds(part * chunk, chunk)]
        pltpu.make_async_remote_copy(
            src_ref=rows,
            dst_ref=rows,
            send_sem=block_send.at[lane],
            recv_sem=block_recv.at[flow if flow <= AFTER else flow + part],
            device_id=where,
            device_id_type=pl.DeviceIdType.MESH,
        ).start()

    def waiter(held, send_sem, recv_sem):
        return pltpu.make_async_remote_copy(
            src_ref=held,
            dst_ref=held,
            send_sem=send_sem,
            recv_sem=recv_sem,
            device_id=sibling_device,
            device_id_type=pl.DeviceIdType.MESH,
        )

    def sent(lane, count):
        waiter(
            blocks_ref.at[0, pl.ds(0, count)], block_send.at[lane], block_recv.at[0]
        ).wait_send()

    def arrive(flow, part, at_line, at_row):
        rows = blocks_ref.at[at_line, at_row, pl.ds(part * chunk, chunk)]
        waiter(rows, block_send.at[0], block_recv.at[flow + part]).wait_recv()

    def arrived(flow, at_line, at_row):
        waiter(
            blocks_ref.at[at_line, at_row], block_send.at[0], block_recv.at[flow]
        ).wait_recv()

    def detour_out(part):
        rows = pl.ds(part * chunk, chunk)
        pltpu.make_async_remote_copy(
            src_ref=blocks_ref.at[line, row, rows],
            dst_ref=detour_ref.at[rows],
            send_sem=block_send.at[0],
            recv_sem=detour_recv.at[part],
            device_id=other_plane(row),
            device_id_type=pl.DeviceIdType.MESH,
        ).start()

    def detour_on(part):
        rows = pl.ds(part * chunk, chunk)
        waiter(detour_ref.at[rows], block_send.at[0], detour_recv.at[part]).wait_recv()
        pltpu.make_async_remote_copy(
            src_ref=detour_ref.at[rows],
            dst_ref=blocks_ref.at[line, hub - 1, rows],
            send_sem=block_send.at[2],
            recv_sem=block_recv.at[NEAR + part],
            device_id=other_plane(hub - 1),
            device_id_type=pl.DeviceIdType.MESH,
        ).start()

    def tell_ids(where):
        pltpu.make_async_remote_copy(
            src_ref=ids_ref.at[me],
            dst_ref=ids_ref.at[me],
            send_sem=ids_send,
            recv_sem=ids_recv,
            device_id=where,
            device_id_type=pl.DeviceIdType.MESH,
        ).start()

    def told_ids(count):
        waiter(ids_ref.at[pl.ds(0, count)], ids_send, ids_recv).wait_send()

    def hear_ids(count):
        waiter(ids_ref.at[pl.ds(0, count)], ids_send, ids_recv).wait_recv()

    def give(at_row, at_col, at_core, best):
        at = spot(at_col * CORES + at_core, at_row)
        given_ref[at] = best
        pltpu.make_async_remote_copy(
            src_ref=given_ref.at[at],
            dst_ref=taken_ref.at[me],
            send_sem=best_send,
            recv_sem=best_recv,
            device_id=device(at_row, at_col, at_core),
            device_id_type=pl.DeviceIdType.MESH,
        ).start()

    def gave(count):
        waiter(given_ref.at[pl.ds(0, count)], best_send, best_recv).wait_send()

    def take(*places):
        with jax.named_scope("w_back"):
            waiter(given_ref.at[pl.ds(0, len(places))], best_send, best_recv).wait_recv()
        best = taken_ref[spot(places[0][0], places[0][1])]
        for at_line, at_row in places[1:]:
            best = jnp.maximum(best, taken_ref[spot(at_line, at_row)])
        return best

    def finish(best):
        out_ref[...] = jnp.where(best > SAME / 2, jnp.maximum(best - SAME, -1.0), -1.0)

    def mark(at_line, at_row):
        shape = (row_count, row_count)
        down = jnp.transpose(jnp.broadcast_to(ids_ref[spot(at_line, at_row)], shape))
        here = down == lax.broadcasted_iota(jnp.int32, shape, 1)
        marks_ref[at_line, at_row] = jnp.where(here, SAME**0.5, 0.0).astype(jnp.bfloat16)

    def flat(ref, *index):
        values = ref[index]
        return values.reshape(-1, values.shape[-1])

    def operand(*indices):
        return jnp.concatenate(
            [
                jnp.concatenate([flat(blocks_ref, *index), flat(marks_ref, *index)], axis=1)
                for index in indices
            ],
            axis=0,
        )

    def scores(left, right):
        return lax.dot_general(
            left, right, (((1,), (1,)), ((), ())), preferred_element_type=jnp.float32
        )

    def down_max(values):
        return jnp.max(values, axis=0, keepdims=True)

    def fold(values):
        folded = values[:, :row_count]
        for at in range(1, values.shape[1] // row_count):
            folded = jnp.maximum(folded, values[:, at * row_count : (at + 1) * row_count])
        return folded

    def turn_max(folded):
        return down_max(jnp.transpose(folded))

    def without_self(values, start):
        down = lax.broadcasted_iota(jnp.int32, values.shape, 0)
        return jnp.where(
            down == lax.broadcasted_iota(jnp.int32, values.shape, 1) + start, -1.0, values
        )

    chip = pl.ds(col * CORES, CORES)

    def split(values):
        low, high = values[:, :row_count], values[:, row_count:]
        return jnp.where(core == 0, low, high), jnp.where(core == 0, high, low)

    def own_best():
        return down_max(
            without_self(scores(operand((chip, row)), operand((line, row))), core * row_count)
        )

    for copy in small_copies:
        copy.wait()
    counts = jnp.transpose(
        jnp.broadcast_to(lengths_ref[...].astype(jnp.float32), (row_count, row_count))
    )[:, 0:1]
    states_copy.wait()
    states = states_ref[...]
    summed = states[:, 0, :].astype(jnp.float32)
    for position in range(1, seq_len):
        token = states[:, position, :].astype(jnp.float32)
        summed = summed + jnp.where(counts > position, token, 0.0)
    pooled = (summed / counts).astype(jnp.bfloat16)
    weight_copy.wait()
    hidden = jnp.tanh(
        jnp.dot(pooled, weight_ref[...], preferred_element_type=jnp.float32) + bias_ref[...]
    )
    factor = lax.rsqrt(jnp.sum(hidden * hidden, axis=1, keepdims=True) + 1e-06)
    blocks_ref[line, row] = (hidden * factor).astype(jnp.bfloat16)

    with jax.named_scope("w_barrier"):
        pl.semaphore_wait(barrier, greetings)

    each_to(tell_ids)

    @pl.when((row != hub) & jnp.logical_not(around))
    def _():
        flow = jnp.where(row == 0, END, jnp.where(row == 1, NEAR, OUTER))
        for part in range(CHUNKS):
            rows = blocks_ref.at[line, row, pl.ds(part * chunk, chunk)]
            pltpu.make_async_remote_copy(
                src_ref=rows,
                dst_ref=rows,
                send_sem=block_send.at[0],
                recv_sem=block_recv.at[flow + part],
                device_id=device(hub, col, core),
                device_id_type=pl.DeviceIdType.MESH,
            ).start()

    @pl.when((row != hub) & around)
    def _():
        for part in range(CHUNKS):
            detour_out(part)

    for part in range(CHUNKS):
        send(ACROSS, part, line, row, device(row, far_col, core))
    for part in range(CHUNKS):
        send(SIBLING, part, line, row, sibling_device)
    mark(line, row)

    @pl.when(row != hub)
    def _():
        for part in range(CHUNKS):
            arrive(ACROSS, part, across_line, row)

            @pl.when(row == 1)
            def _():
                send(AFTER, part, across_line, row, device(0, col, core), 1)

            @pl.when((row > hub) & (core == 0))
            def _():
                send(CORNER, part, across_line, row, device(hub, col, core), 1)

        arrived(SIBLING, sibling_line, row)

        @pl.when(row > 0)
        def _():
            hear_ids(2)

        @pl.when(row == 0)
        def _():
            hear_ids(3)

        mark(across_line, row)
        mark(sibling_line, row)
        both = operand((chip, row))
        mine, other = split(down_max(scores(operand((across_line, row)), both)))
        best_ref[0:1] = jnp.maximum(mine, own_best())
        best_ref[1:2] = other

        @pl.when(row == 0)
        def _():
            with jax.named_scope("w_after"):
                arrived(AFTER, across_line, 1)
            mark(across_line, 1)
            after = scores(operand((across_line, 1)), operand((chip, row)))
            give(1, far_col, core, turn_max(fold(after)))
            mine, other = split(down_max(after))
            best_ref[0:1] = jnp.maximum(best_ref[0:1], mine)
            best_ref[1:2] = jnp.maximum(best_ref[1:2], other)

        give(row, col, far_core, best_ref[1:2])
        sent(0, 3)
        hubs = tuple((col * CORES + at_core, hub) for at_core in range(CORES))

        @pl.when(row == 0)
        def _():
            told_ids(4)
            gave(2)
            finish(jnp.maximum(best_ref[0:1], take((sibling_line, row), *hubs)))

        @pl.when(row == 1)
        def _():
            told_ids(5)
            gave(1)
            sent(1, 1)
            finish(
                jnp.maximum(best_ref[0:1], take((sibling_line, row), (across_line, 0), *hubs))
            )

        @pl.when(row > hub)
        def _():
            told_ids(4)
            gave(1)

            @pl.when(core == 0)
            def _():
                sent(1, 1)

            finish(
                jnp.maximum(best_ref[0:1], take((sibling_line, row), (line, hub), (across_line, hub)))
            )

    @pl.when(row == hub)
    def _():
        outer, beside, corner = (line, hub + 1), (across_line, hub), (across_line, hub + 1)
        near, end = (line, hub - 1), (line, 0)
        near_too, end_too = [(sibling_line, at) for at in (hub - 1, 0)]
        width = CORES * row_count

        def detour(part):
            @pl.when(around)
            def _():
                detour_on(part)

        def pass_outer(part):
            arrive(OUTER, part, *outer)

            @pl.when(core == 1)
            def _():
                send(CORNER, part, *outer, device(hub, far_col, core), 2)

        def pass_near(part):
            arrive(NEAR, part, *near)
            send(NEAR_TOO, part, *near, sibling_device, 1)

        def pass_end(part):
            arrive(END, part, *end)
            send(END_TOO, part, *end, sibling_device, 1)

        def pick(values, at):
            low, high = [
                values[:, (2 * at_core + at) * row_count : (2 * at_core + at + 1) * row_count]
                for at_core in range(CORES)
            ]
            return jnp.where(core == 0, low, high), jnp.where(core == 0, high, low)

        with jax.named_scope("w_a"):
            for part in range(2):
                detour(part)
                pass_outer(part)
                pass_end(part)
        with jax.named_scope("w_ids"):
            hear_ids(8)
        for at_row in range(hub + 1):
            mark(sibling_line, at_row)
        for place in (outer, near, end, beside, corner):
            mark(*place)
        with jax.named_scope("w_b"):
            for part in range(2, CHUNKS):
                detour(part)
                pass_outer(part)
                pass_end(part)
        arrived(SIBLING, sibling_line, hub)
        with jax.named_scope("w_near1"):
            for part in range(2):
                pass_near(part)
        with jax.named_scope("w_beside"):
            for part in range(CHUNKS):
                arrive(ACROSS, part, *beside)
        with jax.named_scope("w_end_too"):
            arrived(END_TOO, *end_too)
        mine_first = operand((line, hub), outer, beside)
        early = scores(mine_first, operand((chip, hub), (chip, 0)))
        own = without_self(early[:row_count, : CORES * row_count], -core * row_count)
        early = jnp.concatenate(
            [jnp.concatenate([own, early[:row_count, CORES * row_count :]], axis=1), early[row_count:]],
            axis=0,
        )
        early_best = down_max(early)
        folded_ref[...] = fold(early)
        with jax.named_scope("w_near"):
            for part in range(2, CHUNKS):
                pass_near(part)
        with jax.named_scope("w_near_too"):
            arrived(NEAR_TOO, *near_too)
        near_scores = scores(operand((line, hub), outer, beside, end), operand((chip, hub - 1)))
        near_best = down_max(near_scores)
        folded = jnp.maximum(folded_ref[...], fold(near_scores[: 3 * row_count]))
        best_ref[0:1] = turn_max(folded[:row_count])
        give(hub + 1, col, core, turn_max(folded[row_count : 2 * row_count]))
        give(hub, far_col, core, turn_max(folded[2 * row_count :]))
        end_best = turn_max(fold(near_scores[3 * row_count :]))
        with jax.named_scope("w_corner"):
            arrived(CORNER, *corner)
        corner_scores = scores(operand(corner), operand((chip, hub), (chip, 0), (chip, hub - 1)))
        last = down_max(corner_scores)
        hub_mine, hub_other = split(jnp.maximum(early_best, last[:, : 2 * width])[:, :width])
        end_mine, end_other = split(jnp.maximum(early_best, last[:, : 2 * width])[:, width:])
        near_mine, near_other = split(jnp.maximum(near_best, last[:, 2 * width :]))
        give(0, col, core, jnp.maximum(end_best, end_mine))
        give(0, col, far_core, end_other)
        give(hub - 1, col, core, near_mine)
        give(hub - 1, col, far_core, near_other)
        give(hub, col, far_core, hub_other)
        give(hub + 1, far_col, core, turn_max(fold(corner_scores)))
        best_ref[0:1] = jnp.maximum(best_ref[0:1], hub_mine)
        sent(0, 2)
        sent(1, 2)

        @pl.when(core == 1)
        def _():
            sent(2, 2)

        told_ids(2)
        gave(8)
        finish(jnp.maximum(best_ref[0:1], take((sibling_line, hub), (across_line, hub))))


def meet_body(token_states, lengths, cluster_id, proj_weight, proj_bias):
    row_count, seq_len, feat_dim = token_states.shape
    lines = lax.axis_size("docs") // ROWS * CORES
    vmem = pl.BlockSpec(memory_space=pltpu.VMEM)
    hbm = pl.BlockSpec(memory_space=pl.ANY)
    result = pl.pallas_call(
        meet_kernel,
        out_shape=pltpu.VMEM((1, row_count), jnp.float32),
        in_specs=[hbm] * 5,
        out_specs=vmem,
        scratch_shapes=[
            pltpu.VMEM((1, row_count), jnp.int32),
            pltpu.VMEM((1, feat_dim), jnp.float32),
            pltpu.VMEM(token_states.shape, jnp.bfloat16),
            pltpu.VMEM(proj_weight.shape, jnp.bfloat16),
            pltpu.VMEM((lines * ROWS, 1, row_count), jnp.int32),
            pltpu.VMEM((lines, ROWS, row_count, feat_dim), jnp.bfloat16),
            pltpu.VMEM((lines, ROWS, row_count, row_count), jnp.bfloat16),
            pltpu.VMEM((row_count, feat_dim), jnp.bfloat16),
            pltpu.VMEM((2, row_count), jnp.float32),
            pltpu.VMEM((3 * row_count, row_count), jnp.float32),
            pltpu.VMEM((lines * ROWS, 1, row_count), jnp.float32),
            pltpu.VMEM((lines * ROWS, 1, row_count), jnp.float32),
            pltpu.SemaphoreType.DMA((3,)),
            pltpu.SemaphoreType.DMA,
            pltpu.SemaphoreType.DMA,
            pltpu.SemaphoreType.DMA((3,)),
            pltpu.SemaphoreType.DMA((FLOWS,)),
            pltpu.SemaphoreType.DMA((CHUNKS,)),
            pltpu.SemaphoreType.DMA,
            pltpu.SemaphoreType.DMA,
            pltpu.SemaphoreType.DMA,
            pltpu.SemaphoreType.DMA,
        ],
        compiler_params=pltpu.CompilerParams(collective_id=0, has_side_effects=True),
        name="scores",
    )(token_states, lengths[None, :], cluster_id[None, :], proj_weight, proj_bias[None, :])
    return result.reshape(row_count)

def solution(mesh):
    in_specs = (
        P(("groups", "docs", "help"), None, None),
        P(("groups", "docs", "help")),
        P(("groups", "docs", "help")),
        P(),
        P(),
    )
    out_specs = P(("groups", "docs", "help"))
    meets = mesh.shape["docs"] == 2 * ROWS and mesh.shape["help"] == CORES and mesh.shape["groups"] == 2
    return jax.shard_map(meet_body if meets else body, mesh=mesh, in_specs=in_specs, out_specs=out_specs, check_vma=False)
```

```python
import jax
import jax.numpy as jnp
from jax import lax
from jax.experimental import pallas as pl
from jax.experimental.pallas import tpu as pltpu
from jax.sharding import PartitionSpec as P

CL_OWN = 1


def partner(value, axis, bit):
    return lax.ppermute(value, axis, [(i, i ^ 1 << bit) for i in range(lax.axis_size(axis))])


def slot_maxima(own_emb, own_ids, self_pos, col_emb, col_ids):
    row_total = own_emb.shape[0]
    block = min(row_total, 512)
    col_pos = lax.broadcasted_iota(jnp.int32, (col_emb.shape[0],), 0)

    def block_max(pieces):
        part_emb, part_ids, part_self = pieces
        duplicate_scores = jnp.einsum(
            "rd,cd->rc", part_emb, col_emb, preferred_element_type=jnp.float32
        )
        match = (
            (part_ids[:, None] == col_ids[None, :])
            & (col_ids[None, :] >= 0)
            & (part_self[:, None] != col_pos[None, :])
        )
        return jnp.max(jnp.where(match, duplicate_scores, -1.0), axis=1)

    steps_count = row_total // block
    result = lax.map(
        block_max,
        (
            own_emb.reshape(steps_count, block, own_emb.shape[1]),
            own_ids.reshape(steps_count, block),
            self_pos.reshape(steps_count, block),
        ),
    )
    return result.reshape(row_total)


def body(token_states, lengths, cluster_id, proj_weight, proj_bias):
    row_count, seq_len, feat_dim = token_states.shape
    owners = lax.axis_size("docs")
    slot_cap = 2 * row_count // owners
    position_count = owners * slot_cap
    token_mask = (
        lax.broadcasted_iota(jnp.int32, (row_count, seq_len), 1) < lengths[:, None]
    ).astype(jnp.bfloat16)
    summed = jnp.einsum("rsd,rs->rd", token_states, token_mask, preferred_element_type=jnp.float32)
    pooled = (summed / lengths[:, None].astype(jnp.float32)).astype(jnp.bfloat16)
    hidden = jnp.tanh(jnp.dot(pooled, proj_weight, preferred_element_type=jnp.float32) + proj_bias)
    factor = lax.rsqrt(jnp.sum(hidden * hidden, axis=1, keepdims=True) + 1e-06)
    embedded = (hidden * factor).astype(jnp.bfloat16)
    dest_owner = cluster_id // CL_OWN
    same_owner = dest_owner[:, None] == dest_owner[None, :]
    earlier = lax.broadcasted_iota(jnp.int32, (row_count, row_count), 1) < lax.broadcasted_iota(
        jnp.int32, (row_count, row_count), 0
    )
    slot_rank = jnp.sum((same_owner & earlier).astype(jnp.int32), axis=1)
    target = dest_owner * slot_cap + slot_rank
    chooser = lax.broadcasted_iota(jnp.int32, (position_count, row_count), 0) == target[None, :]
    packed = jnp.dot(
        chooser.astype(jnp.bfloat16), embedded, preferred_element_type=jnp.float32
    ).astype(jnp.bfloat16)
    packed_ids = jnp.max(jnp.where(chooser, cluster_id[None, :], -1), axis=1)
    own_emb, own_ids = (
        lax.all_to_all(packed, "docs", split_axis=0, concat_axis=0, tiled=True),
        lax.all_to_all(packed_ids, "docs", split_axis=0, concat_axis=0, tiled=True),
    )
    mate_emb, mate_ids = partner((own_emb, own_ids), "help", 0)
    col_emb = jnp.concatenate([own_emb, mate_emb], axis=0)
    col_ids = jnp.concatenate([own_ids, mate_ids], axis=0)
    self_pos = lax.broadcasted_iota(jnp.int32, (position_count,), 0)
    maxima = slot_maxima(own_emb, own_ids, self_pos, col_emb, col_ids)
    returned = lax.all_to_all(maxima, "docs", split_axis=0, concat_axis=0, tiled=True)
    return jnp.max(jnp.where(chooser, returned[:, None], -3.0), axis=0)


ROWS = 4
CORES = 2
CHUNKS = 4
SLABS = 2
KEPT = 4
ROUND = 1
SAME = 4.0
SIBLING, CORNER, NEAR_TOO, END_TOO, OUTER_TOO, BESIDE_TOO, AFTER = range(7)
ACROSS, OUTER, NEAR, END = (AFTER + 1 + CHUNKS * at for at in range(4))
FLOWS = END + CHUNKS


def meet_kernel(
    states_hbm,
    lengths_hbm,
    ids_hbm,
    weight_hbm,
    bias_hbm,
    out_ref,
    lengths_ref,
    bias_ref,
    states_ref,
    weight_ref,
    ids_ref,
    blocks_ref,
    marks_ref,
    detour_ref,
    best_ref,
    folded_ref,
    given_ref,
    taken_ref,
    small_sem,
    states_sem,
    weight_sem,
    block_send,
    block_recv,
    detour_recv,
    ids_send,
    ids_recv,
    best_send,
    best_recv,
):
    row_count, seq_len, feat_dim = states_ref.shape
    lines = blocks_ref.shape[0]
    columns = lines // CORES
    chunk = row_count // CHUNKS
    hub = ROWS - 2
    group = lax.axis_index("groups")
    docs = lax.axis_index("docs")
    core = lax.axis_index("help")
    depth = docs // columns
    col = docs % columns
    row = depth + group * (ROWS - 1 - 2 * depth)
    far_col = columns - 1 - col
    far_core = CORES - 1 - core
    line = col * CORES + core
    sibling_line = col * CORES + far_core
    across_line = far_col * CORES + core

    def device(at_row, at_col, at_core):
        at_depth = at_row + group * (ROWS - 1 - 2 * at_row)
        return {"docs": at_depth * columns + at_col, "help": at_core}

    def other_plane(at_row):
        at_depth = at_row + group * (ROWS - 1 - 2 * at_row)
        return {"groups": 1 - group, "docs": at_depth * columns + col, "help": core}

    def spot(at_line, at_row):
        return at_line * ROWS + at_row

    me = spot(line, row)
    sibling_device = device(row, col, far_core)

    small_copies = [
        pltpu.make_async_copy(source, held, small_sem.at[position])
        for position, (source, held) in enumerate(
            [(lengths_hbm, lengths_ref), (ids_hbm, ids_ref.at[me]), (bias_hbm, bias_ref)]
        )
    ]
    for copy in small_copies:
        copy.start()
    states_copy = pltpu.make_async_copy(states_hbm, states_ref, states_sem)
    states_copy.start()
    slab = feat_dim // SLABS
    weight_copies = [
        pltpu.make_async_copy(
            weight_hbm.at[pl.ds(at * slab, slab)],
            weight_ref.at[pl.ds(at * slab, slab)],
            weight_sem.at[at],
        )
        for at in range(SLABS)
    ]
    for copy in weight_copies:
        copy.start()

    barrier = pltpu.get_barrier_semaphore()

    def greet(*wheres):
        for where in wheres:
            pl.semaphore_signal(
                barrier, inc=1, device_id=where, device_id_type=pl.DeviceIdType.MESH
            )

    around = (core == 1) | (group == 1)
    passing = (core == 1) | (group == 0)

    def each_to(act):
        @pl.when(row != hub)
        def _():
            for at_core in range(CORES):
                act(device(hub, col, at_core))

        @pl.when(row == 1)
        def _():
            act(device(0, far_col, core))

        @pl.when(row == hub)
        def _():
            act(device(hub, far_col, far_core))

        @pl.when(row > hub)
        def _():
            act(device(hub, far_col, core))

        act(device(row, far_col, core))
        act(sibling_device)

    each_to(lambda where: greet(where))

    @pl.when(row == 0)
    def _():
        greet(device(1, col, core), device(1, far_col, core))

    @pl.when(row == 1)
    def _():
        greet(device(0, col, core))

    @pl.when(row == hub)
    def _():
        for at_row in (0, 1, hub + 1):
            for at_core in range(CORES):
                greet(device(at_row, col, at_core))
        greet(device(hub + 1, far_col, core))

    @pl.when((row == 1) & around)
    def _():
        greet(other_plane(row))

    @pl.when((row == hub) & passing)
    def _():
        greet(other_plane(row), other_plane(hub - 1))

    @pl.when((row == hub) & around & jnp.logical_not((core == 1) & passing))
    def _():
        greet(other_plane(hub - 1))

    greetings = (
        2
        + 4 * (row < hub)
        + 8 * (row == hub)
        + 3 * (row > hub)
        + ((row == 1) & around)
        + (row == hub) * (1 + passing)
    )

    def send(flow, part, at_line, at_row, where, lane=0):
        rows = blocks_ref.at[at_line, at_row, pl.ds(part * chunk, chunk)]
        pltpu.make_async_remote_copy(
            src_ref=rows,
            dst_ref=rows,
            send_sem=block_send.at[lane],
            recv_sem=block_recv.at[flow if flow <= AFTER else flow + part],
            device_id=where,
            device_id_type=pl.DeviceIdType.MESH,
        ).start()

    def waiter(held, send_sem, recv_sem):
        return pltpu.make_async_remote_copy(
            src_ref=held,
            dst_ref=held,
            send_sem=send_sem,
            recv_sem=recv_sem,
            device_id=sibling_device,
            device_id_type=pl.DeviceIdType.MESH,
        )

    def sent(lane, count):
        waiter(
            blocks_ref.at[0, pl.ds(0, count)], block_send.at[lane], block_recv.at[0]
        ).wait_send()

    def sent_parts(lane, count):
        rows = blocks_ref.at[0, 0, pl.ds(0, count * chunk)]
        waiter(rows, block_send.at[lane], block_recv.at[0]).wait_send()

    def arrive(flow, part, at_line, at_row):
        rows = blocks_ref.at[at_line, at_row, pl.ds(part * chunk, chunk)]
        waiter(rows, block_send.at[0], block_recv.at[flow + part]).wait_recv()

    def arrived(flow, at_line, at_row):
        waiter(
            blocks_ref.at[at_line, at_row], block_send.at[0], block_recv.at[flow]
        ).wait_recv()

    def detour_out(part):
        rows = pl.ds(part * chunk, chunk)
        pltpu.make_async_remote_copy(
            src_ref=blocks_ref.at[line, row, rows],
            dst_ref=detour_ref.at[rows],
            send_sem=block_send.at[0],
            recv_sem=detour_recv.at[part],
            device_id=other_plane(row),
            device_id_type=pl.DeviceIdType.MESH,
        ).start()

    def detour_on(part):
        rows = pl.ds(part * chunk, chunk)
        waiter(detour_ref.at[rows], block_send.at[0], detour_recv.at[part]).wait_recv()
        pltpu.make_async_remote_copy(
            src_ref=detour_ref.at[rows],
            dst_ref=blocks_ref.at[line, hub - 1, rows],
            send_sem=block_send.at[3],
            recv_sem=block_recv.at[NEAR + part],
            device_id=other_plane(hub - 1),
            device_id_type=pl.DeviceIdType.MESH,
        ).start()

    def tell_ids(where):
        pltpu.make_async_remote_copy(
            src_ref=ids_ref.at[me],
            dst_ref=ids_ref.at[me],
            send_sem=ids_send,
            recv_sem=ids_recv,
            device_id=where,
            device_id_type=pl.DeviceIdType.MESH,
        ).start()

    def told_ids(count):
        waiter(ids_ref.at[pl.ds(0, count)], ids_send, ids_recv).wait_send()

    def hear_ids(count):
        waiter(ids_ref.at[pl.ds(0, count)], ids_send, ids_recv).wait_recv()

    def give(at_row, at_col, at_core, best):
        at = spot(at_col * CORES + at_core, at_row)
        given_ref[at] = best
        pltpu.make_async_remote_copy(
            src_ref=given_ref.at[at],
            dst_ref=taken_ref.at[me],
            send_sem=best_send,
            recv_sem=best_recv,
            device_id=device(at_row, at_col, at_core),
            device_id_type=pl.DeviceIdType.MESH,
        ).start()

    def gave(count):
        waiter(given_ref.at[pl.ds(0, count)], best_send, best_recv).wait_send()

    def take(*places):
        with jax.named_scope("w_back"):
            waiter(given_ref.at[pl.ds(0, len(places))], best_send, best_recv).wait_recv()
        best = taken_ref[spot(places[0][0], places[0][1])]
        for at_line, at_row in places[1:]:
            best = jnp.maximum(best, taken_ref[spot(at_line, at_row)])
        return best

    def finish(best):
        out_ref[...] = jnp.where(best > SAME / 2, jnp.maximum(best - SAME, -1.0), -1.0)

    def mark(at_line, at_row):
        shape = (row_count, row_count)
        down = jnp.transpose(jnp.broadcast_to(ids_ref[spot(at_line, at_row)], shape))
        here = down == lax.broadcasted_iota(jnp.int32, shape, 1)
        marks_ref[at_line, at_row] = jnp.where(here, SAME**0.5, 0.0).astype(jnp.bfloat16)

    def flat(ref, *index):
        values = ref[index]
        return values.reshape(-1, values.shape[-1])

    def operand(*indices):
        return jnp.concatenate(
            [
                jnp.concatenate([flat(blocks_ref, *index), flat(marks_ref, *index)], axis=1)
                for index in indices
            ],
            axis=0,
        )

    def scores(left, right):
        return lax.dot_general(
            left, right, (((1,), (1,)), ((), ())), preferred_element_type=jnp.float32
        )

    def down_max(values):
        return jnp.max(values, axis=0, keepdims=True)

    def fold(values):
        folded = values[:, :row_count]
        for at in range(1, values.shape[1] // row_count):
            folded = jnp.maximum(folded, values[:, at * row_count : (at + 1) * row_count])
        return folded

    def turn_max(folded):
        return down_max(jnp.transpose(folded))

    def without_self(values, start):
        down = lax.broadcasted_iota(jnp.int32, values.shape, 0)
        return jnp.where(
            down == lax.broadcasted_iota(jnp.int32, values.shape, 1) + start, -1.0, values
        )

    chip = pl.ds(col * CORES, CORES)

    def split(values):
        low, high = values[:, :row_count], values[:, row_count:]
        return jnp.where(core == 0, low, high), jnp.where(core == 0, high, low)

    def own_best():
        return down_max(
            without_self(scores(operand((chip, row)), operand((line, row))), core * row_count)
        )

    for copy in small_copies:
        copy.wait()
    counts = jnp.transpose(
        jnp.broadcast_to(lengths_ref[...].astype(jnp.float32), (row_count, row_count))
    )[:, 0:1]
    states_copy.wait()
    states = states_ref[...]
    summed = states[:, 0, :].astype(jnp.float32)
    for position in range(1, seq_len):
        token = states[:, position, :].astype(jnp.float32)
        summed = summed + jnp.where(counts > position, token, 0.0)
    pooled = (summed / counts).astype(jnp.bfloat16)
    projected = bias_ref[...]
    for at, copy in enumerate(weight_copies):
        copy.wait()
        depth_at = slice(at * slab, (at + 1) * slab)
        projected = projected + jnp.dot(
            pooled[:, depth_at], weight_ref[depth_at], preferred_element_type=jnp.float32
        )
    hidden = jnp.tanh(projected)
    factor = lax.rsqrt(jnp.sum(hidden * hidden, axis=1, keepdims=True) + 1e-06)
    blocks_ref[line, row] = (hidden * factor).astype(jnp.bfloat16)

    with jax.named_scope("w_barrier"):
        pl.semaphore_wait(barrier, greetings)

    each_to(tell_ids)

    flow = jnp.where(row == 0, END, jnp.where(row == 1, NEAR, OUTER))
    for part in range(CHUNKS):
        if part < CHUNKS - ROUND:
            detours = (row == 1) & (core == 1)
        else:
            detours = (row == 1) & around

        @pl.when((row != hub) & jnp.logical_not(detours))
        def _():
            rows = blocks_ref.at[line, row, pl.ds(part * chunk, chunk)]
            pltpu.make_async_remote_copy(
                src_ref=rows,
                dst_ref=rows,
                send_sem=block_send.at[0],
                recv_sem=block_recv.at[flow + part],
                device_id=device(hub, col, core),
                device_id_type=pl.DeviceIdType.MESH,
            ).start()

        @pl.when(detours)
        def _():
            detour_out(part)

    for part in range(CHUNKS):
        send(SIBLING, part, line, row, sibling_device, 4)

    def send_across():
        for part in range(CHUNKS):
            send(ACROSS, part, line, row, device(row, far_col, core), 4)

    later = (row > hub) & (core == 1)

    @pl.when(jnp.logical_not(later))
    def _():
        send_across()

    mark(line, row)

    @pl.when(later)
    def _():
        sent(0, 1)
        send_across()

    @pl.when(row != hub)
    def _():
        for part in range(CHUNKS):
            arrive(ACROSS, part, across_line, row)

            @pl.when(row == 1)
            def _():
                send(AFTER, part, across_line, row, device(0, col, core), 1)

            if part < KEPT:

                @pl.when((row > hub) & (core == 0))
                def _():
                    send(CORNER, part, across_line, row, device(hub, col, core), 1)

        arrived(SIBLING, sibling_line, row)

        @pl.when(row > 0)
        def _():
            hear_ids(2)

        @pl.when(row == 0)
        def _():
            hear_ids(3)

        mark(across_line, row)
        mark(sibling_line, row)
        both = operand((chip, row))
        mine, other = split(down_max(scores(operand((across_line, row)), both)))
        best_ref[0:1] = jnp.maximum(mine, own_best())
        best_ref[1:2] = other

        @pl.when(row == 0)
        def _():
            with jax.named_scope("w_after"):
                arrived(AFTER, across_line, 1)
            mark(across_line, 1)
            after = scores(operand((across_line, 1)), operand((chip, row)))
            give(1, far_col, core, turn_max(fold(after)))
            mine, other = split(down_max(after))
            best_ref[0:1] = jnp.maximum(best_ref[0:1], mine)
            best_ref[1:2] = jnp.maximum(best_ref[1:2], other)

        give(row, col, far_core, best_ref[1:2])
        sent(4, 2)

        @pl.when(jnp.logical_not(later))
        def _():
            sent(0, 1)

        hubs = tuple((col * CORES + at_core, hub) for at_core in range(CORES))

        @pl.when(row == 0)
        def _():
            told_ids(4)
            gave(2)
            finish(jnp.maximum(best_ref[0:1], take((sibling_line, row), *hubs)))

        @pl.when(row == 1)
        def _():
            told_ids(5)
            gave(1)
            sent(1, 1)
            finish(
                jnp.maximum(best_ref[0:1], take((sibling_line, row), (across_line, 0), *hubs))
            )

        @pl.when(row > hub)
        def _():
            told_ids(5)
            gave(1)

            @pl.when(core == 0)
            def _():
                sent_parts(1, KEPT)

            finish(
                jnp.maximum(best_ref[0:1], take((sibling_line, row), (across_line, hub), *hubs))
            )

    @pl.when(row == hub)
    def _():
        outer, beside, corner = (line, hub + 1), (across_line, hub), (across_line, hub + 1)
        near, end = (line, hub - 1), (line, 0)
        near_too, end_too, outer_too = [(sibling_line, at) for at in (hub - 1, 0, hub + 1)]
        beside_too = (far_col * CORES + far_core, hub)
        far_chip = pl.ds(far_col * CORES, CORES)
        width = CORES * row_count

        def detour(part):
            passes = passing if part >= CHUNKS - ROUND else core == 1

            @pl.when(passes)
            def _():
                detour_on(part)

        def pass_outer(part):
            arrive(OUTER, part, *outer)
            send(OUTER_TOO, part, *outer, sibling_device, 1)

            @pl.when(True if part >= KEPT else core == 1)
            def _():
                send(CORNER, part, *outer, device(hub, far_col, core), 2)

        def pass_near(part):
            arrive(NEAR, part, *near)
            send(NEAR_TOO, part, *near, sibling_device, 1)

        def pass_end(part):
            arrive(END, part, *end)
            send(END_TOO, part, *end, sibling_device, 1)

        def pick(values, at):
            low, high = [
                values[:, (2 * at_core + at) * row_count : (2 * at_core + at + 1) * row_count]
                for at_core in range(CORES)
            ]
            return jnp.where(core == 0, low, high), jnp.where(core == 0, high, low)

        with jax.named_scope("w_a"):
            for part in range(2):
                detour(part)
                pass_outer(part)
                pass_end(part)
        with jax.named_scope("w_ids"):
            hear_ids(10)
        for at_row in range(ROWS):
            mark(sibling_line, at_row)
        for place in (outer, near, end, beside, beside_too, corner):
            mark(*place)
        with jax.named_scope("w_b"):
            for part in range(2, CHUNKS):
                detour(part)
                pass_outer(part)
                pass_end(part)
        arrived(SIBLING, sibling_line, hub)
        with jax.named_scope("w_beside"):
            for part in range(CHUNKS):
                arrive(ACROSS, part, *beside)
                send(BESIDE_TOO, part, *beside, sibling_device, 1)
        with jax.named_scope("w_near1"):
            pass_near(0)
        early = scores(operand((line, hub), outer, beside, end), operand((chip, hub)))
        own = without_self(early[:row_count], -core * row_count)
        hub_best = jnp.maximum(down_max(own), down_max(early[row_count:]))
        folded_ref[...] = fold(early[row_count:])
        with jax.named_scope("w_near"):
            for part in range(1, CHUNKS):
                pass_near(part)
        with jax.named_scope("w_too"):
            arrived(OUTER_TOO, *outer_too)
            arrived(BESIDE_TOO, *beside_too)
            arrived(END_TOO, *end_too)
        right_scores = scores(operand(end, near, beside), operand((chip, hub + 1), (far_chip, hub)))
        end_scores = scores(operand(near), operand((chip, 0)))
        left_size = 2 * row_count
        mine, other = split(down_max(right_scores[:, :width]))
        give(hub + 1, col, far_core, other)
        give(hub + 1, col, core, jnp.maximum(turn_max(folded_ref[:row_count]), mine))
        end_folded = jnp.maximum(folded_ref[2 * row_count :], fold(right_scores[:row_count]))
        near_folded = jnp.maximum(fold(end_scores), fold(right_scores[row_count:left_size]))
        end_best = down_max(end_scores)
        end_turned = turn_max(end_folded)
        beside_folded = jnp.maximum(
            folded_ref[row_count:left_size], fold(right_scores[left_size:, :width])
        )
        beside_best = down_max(right_scores[:left_size, width:])
        with jax.named_scope("w_near_too"):
            arrived(NEAR_TOO, *near_too)
        with jax.named_scope("w_corner"):
            arrived(CORNER, *corner)
        corner_scores = scores(operand(corner), operand((chip, 0), (chip, hub - 1)))
        last = down_max(corner_scores)
        mine, other = split(jnp.maximum(end_best, last[:, :width]))
        give(0, col, core, jnp.maximum(end_turned, mine))
        give(0, col, far_core, other)
        give(hub + 1, far_col, core, turn_max(fold(corner_scores)))
        hub_scores = scores(operand(near), operand((chip, hub)))
        near_mine, near_other = split(last[:, width:])
        give(hub - 1, col, far_core, near_other)
        near_turned = turn_max(jnp.maximum(near_folded, fold(hub_scores)))
        give(hub - 1, col, core, jnp.maximum(near_turned, near_mine))
        mine, other = split(beside_best)
        give(hub, far_col, core, jnp.maximum(turn_max(beside_folded), mine))
        give(hub, far_col, far_core, other)
        hub_mine, hub_other = split(jnp.maximum(hub_best, down_max(hub_scores)))
        give(hub, col, far_core, hub_other)
        best_ref[0:1] = hub_mine
        with jax.named_scope("w_sent"):
            pass
        sent(4, 2)
        sent(1, 4)

        @pl.when(core == 1)
        def _():
            sent(2, 1)
            sent(3, 1)

        @pl.when(core == 0)
        def _():
            pass

        @pl.when((core == 0) & passing)
        def _():
            sent_parts(3, ROUND)

        told_ids(3)
        gave(10)
        finish(jnp.maximum(best_ref[0:1], take((sibling_line, hub), (across_line, hub), beside_too)))


def meet_body(token_states, lengths, cluster_id, proj_weight, proj_bias):
    row_count, seq_len, feat_dim = token_states.shape
    lines = lax.axis_size("docs") // ROWS * CORES
    vmem = pl.BlockSpec(memory_space=pltpu.VMEM)
    hbm = pl.BlockSpec(memory_space=pl.ANY)
    result = pl.pallas_call(
        meet_kernel,
        out_shape=pltpu.VMEM((1, row_count), jnp.float32),
        in_specs=[hbm] * 5,
        out_specs=vmem,
        scratch_shapes=[
            pltpu.VMEM((1, row_count), jnp.int32),
            pltpu.VMEM((1, feat_dim), jnp.float32),
            pltpu.VMEM(token_states.shape, jnp.bfloat16),
            pltpu.VMEM(proj_weight.shape, jnp.bfloat16),
            pltpu.VMEM((lines * ROWS, 1, row_count), jnp.int32),
            pltpu.VMEM((lines, ROWS, row_count, feat_dim), jnp.bfloat16),
            pltpu.VMEM((lines, ROWS, row_count, row_count), jnp.bfloat16),
            pltpu.VMEM((row_count, feat_dim), jnp.bfloat16),
            pltpu.VMEM((2, row_count), jnp.float32),
            pltpu.VMEM((3 * row_count, row_count), jnp.float32),
            pltpu.VMEM((lines * ROWS, 1, row_count), jnp.float32),
            pltpu.VMEM((lines * ROWS, 1, row_count), jnp.float32),
            pltpu.SemaphoreType.DMA((3,)),
            pltpu.SemaphoreType.DMA,
            pltpu.SemaphoreType.DMA((SLABS,)),
            pltpu.SemaphoreType.DMA((5,)),
            pltpu.SemaphoreType.DMA((FLOWS,)),
            pltpu.SemaphoreType.DMA((CHUNKS,)),
            pltpu.SemaphoreType.DMA,
            pltpu.SemaphoreType.DMA,
            pltpu.SemaphoreType.DMA,
            pltpu.SemaphoreType.DMA,
        ],
        compiler_params=pltpu.CompilerParams(collective_id=0, has_side_effects=True),
        name="scores",
    )(token_states, lengths[None, :], cluster_id[None, :], proj_weight, proj_bias[None, :])
    return result.reshape(row_count)

def solution(mesh):
    in_specs = (
        P(("groups", "docs", "help"), None, None),
        P(("groups", "docs", "help")),
        P(("groups", "docs", "help")),
        P(),
        P(),
    )
    out_specs = P(("groups", "docs", "help"))
    meets = mesh.shape["docs"] == 2 * ROWS and mesh.shape["help"] == CORES and mesh.shape["groups"] == 2
    return jax.shard_map(meet_body if meets else body, mesh=mesh, in_specs=in_specs, out_specs=out_specs, check_vma=False)
```

```python
import jax
import jax.numpy as jnp
from jax import lax
from jax.experimental import pallas as pl
from jax.experimental.pallas import tpu as pltpu
from jax.sharding import PartitionSpec as P

CL_OWN = 1


def partner(value, axis, bit):
    return lax.ppermute(value, axis, [(i, i ^ 1 << bit) for i in range(lax.axis_size(axis))])


def slot_maxima(own_emb, own_ids, self_pos, col_emb, col_ids):
    row_total = own_emb.shape[0]
    block = min(row_total, 512)
    col_pos = lax.broadcasted_iota(jnp.int32, (col_emb.shape[0],), 0)

    def block_max(pieces):
        part_emb, part_ids, part_self = pieces
        duplicate_scores = jnp.einsum(
            "rd,cd->rc", part_emb, col_emb, preferred_element_type=jnp.float32
        )
        match = (
            (part_ids[:, None] == col_ids[None, :])
            & (col_ids[None, :] >= 0)
            & (part_self[:, None] != col_pos[None, :])
        )
        return jnp.max(jnp.where(match, duplicate_scores, -1.0), axis=1)

    steps_count = row_total // block
    result = lax.map(
        block_max,
        (
            own_emb.reshape(steps_count, block, own_emb.shape[1]),
            own_ids.reshape(steps_count, block),
            self_pos.reshape(steps_count, block),
        ),
    )
    return result.reshape(row_total)


def body(token_states, lengths, cluster_id, proj_weight, proj_bias):
    row_count, seq_len, feat_dim = token_states.shape
    owners = lax.axis_size("docs")
    slot_cap = 2 * row_count // owners
    position_count = owners * slot_cap
    token_mask = (
        lax.broadcasted_iota(jnp.int32, (row_count, seq_len), 1) < lengths[:, None]
    ).astype(jnp.bfloat16)
    summed = jnp.einsum("rsd,rs->rd", token_states, token_mask, preferred_element_type=jnp.float32)
    pooled = (summed / lengths[:, None].astype(jnp.float32)).astype(jnp.bfloat16)
    hidden = jnp.tanh(jnp.dot(pooled, proj_weight, preferred_element_type=jnp.float32) + proj_bias)
    factor = lax.rsqrt(jnp.sum(hidden * hidden, axis=1, keepdims=True) + 1e-06)
    embedded = (hidden * factor).astype(jnp.bfloat16)
    dest_owner = cluster_id // CL_OWN
    same_owner = dest_owner[:, None] == dest_owner[None, :]
    earlier = lax.broadcasted_iota(jnp.int32, (row_count, row_count), 1) < lax.broadcasted_iota(
        jnp.int32, (row_count, row_count), 0
    )
    slot_rank = jnp.sum((same_owner & earlier).astype(jnp.int32), axis=1)
    target = dest_owner * slot_cap + slot_rank
    chooser = lax.broadcasted_iota(jnp.int32, (position_count, row_count), 0) == target[None, :]
    packed = jnp.dot(
        chooser.astype(jnp.bfloat16), embedded, preferred_element_type=jnp.float32
    ).astype(jnp.bfloat16)
    packed_ids = jnp.max(jnp.where(chooser, cluster_id[None, :], -1), axis=1)
    own_emb, own_ids = (
        lax.all_to_all(packed, "docs", split_axis=0, concat_axis=0, tiled=True),
        lax.all_to_all(packed_ids, "docs", split_axis=0, concat_axis=0, tiled=True),
    )
    mate_emb, mate_ids = partner((own_emb, own_ids), "help", 0)
    col_emb = jnp.concatenate([own_emb, mate_emb], axis=0)
    col_ids = jnp.concatenate([own_ids, mate_ids], axis=0)
    self_pos = lax.broadcasted_iota(jnp.int32, (position_count,), 0)
    maxima = slot_maxima(own_emb, own_ids, self_pos, col_emb, col_ids)
    returned = lax.all_to_all(maxima, "docs", split_axis=0, concat_axis=0, tiled=True)
    return jnp.max(jnp.where(chooser, returned[:, None], -3.0), axis=0)


ROWS = 4
CORES = 2
CHUNKS = 4
SLABS = 2
KEPT = 4
ROUND = 1
SAME = 4.0
SIBLING, CORNER, NEAR_TOO, END_TOO, OUTER_TOO, BESIDE_TOO, AFTER = range(7)
ACROSS, OUTER, NEAR, END = (AFTER + 1 + CHUNKS * at for at in range(4))
FLOWS = END + CHUNKS


def meet_kernel(
    states_hbm,
    lengths_hbm,
    ids_hbm,
    weight_hbm,
    bias_hbm,
    out_ref,
    lengths_ref,
    bias_ref,
    states_ref,
    weight_ref,
    ids_ref,
    blocks_ref,
    marks_ref,
    detour_ref,
    best_ref,
    folded_ref,
    given_ref,
    taken_ref,
    small_sem,
    states_sem,
    weight_sem,
    block_send,
    block_recv,
    detour_recv,
    ids_send,
    ids_recv,
    best_send,
    best_recv,
):
    row_count, seq_len, feat_dim = states_ref.shape
    lines = blocks_ref.shape[0]
    columns = lines // CORES
    chunk = row_count // CHUNKS
    hub = ROWS - 2
    group = lax.axis_index("groups")
    docs = lax.axis_index("docs")
    core = lax.axis_index("help")
    depth = docs // columns
    col = docs % columns
    row = depth + group * (ROWS - 1 - 2 * depth)
    far_col = columns - 1 - col
    far_core = CORES - 1 - core
    line = col * CORES + core
    sibling_line = col * CORES + far_core
    across_line = far_col * CORES + core

    def device(at_row, at_col, at_core):
        at_depth = at_row + group * (ROWS - 1 - 2 * at_row)
        return {"docs": at_depth * columns + at_col, "help": at_core}

    def other_plane(at_row):
        at_depth = at_row + group * (ROWS - 1 - 2 * at_row)
        return {"groups": 1 - group, "docs": at_depth * columns + col, "help": core}

    def spot(at_line, at_row):
        return at_line * ROWS + at_row

    me = spot(line, row)
    sibling_device = device(row, col, far_core)

    states_copy = pltpu.make_async_copy(states_hbm, states_ref, states_sem)
    states_copy.start()
    small_copies = [
        pltpu.make_async_copy(source, held, small_sem.at[position])
        for position, (source, held) in enumerate(
            [(lengths_hbm, lengths_ref), (ids_hbm, ids_ref.at[me]), (bias_hbm, bias_ref)]
        )
    ]
    for copy in small_copies:
        copy.start()
    slab = feat_dim // SLABS
    weight_copies = [
        pltpu.make_async_copy(
            weight_hbm.at[pl.ds(at * slab, slab)],
            weight_ref.at[pl.ds(at * slab, slab)],
            weight_sem.at[at],
        )
        for at in range(SLABS)
    ]

    barrier = pltpu.get_barrier_semaphore()

    def greet(*wheres):
        for where in wheres:
            pl.semaphore_signal(
                barrier, inc=1, device_id=where, device_id_type=pl.DeviceIdType.MESH
            )

    around = (core == 1) | (group == 1)
    passing = (core == 1) | (group == 0)

    def each_to(act):
        @pl.when(row != hub)
        def _():
            for at_core in range(CORES):
                act(device(hub, col, at_core))

        @pl.when(row == 1)
        def _():
            act(device(0, far_col, core))

        @pl.when(row == hub)
        def _():
            act(device(hub, far_col, far_core))

        @pl.when(row > hub)
        def _():
            act(device(hub, far_col, core))

        act(device(row, far_col, core))
        act(sibling_device)

    each_to(lambda where: greet(where))

    @pl.when(row == 0)
    def _():
        greet(device(1, col, core), device(1, far_col, core))

    @pl.when(row == 1)
    def _():
        greet(device(0, col, core))

    @pl.when(row == hub)
    def _():
        for at_row in (0, 1, hub + 1):
            for at_core in range(CORES):
                greet(device(at_row, col, at_core))
        greet(device(hub + 1, far_col, core))

    @pl.when((row == 1) & around)
    def _():
        greet(other_plane(row))

    @pl.when((row == hub) & passing)
    def _():
        greet(other_plane(row), other_plane(hub - 1))

    @pl.when((row == hub) & around & jnp.logical_not((core == 1) & passing))
    def _():
        greet(other_plane(hub - 1))

    for copy in weight_copies:
        copy.start()

    greetings = (
        2
        + 4 * (row < hub)
        + 8 * (row == hub)
        + 3 * (row > hub)
        + ((row == 1) & around)
        + (row == hub) * (1 + passing)
    )

    def send(flow, part, at_line, at_row, where, lane=0):
        rows = blocks_ref.at[at_line, at_row, pl.ds(part * chunk, chunk)]
        pltpu.make_async_remote_copy(
            src_ref=rows,
            dst_ref=rows,
            send_sem=block_send.at[lane],
            recv_sem=block_recv.at[flow if flow <= AFTER else flow + part],
            device_id=where,
            device_id_type=pl.DeviceIdType.MESH,
        ).start()

    def waiter(held, send_sem, recv_sem):
        return pltpu.make_async_remote_copy(
            src_ref=held,
            dst_ref=held,
            send_sem=send_sem,
            recv_sem=recv_sem,
            device_id=sibling_device,
            device_id_type=pl.DeviceIdType.MESH,
        )

    def sent(lane, count):
        waiter(
            blocks_ref.at[0, pl.ds(0, count)], block_send.at[lane], block_recv.at[0]
        ).wait_send()

    def sent_parts(lane, count):
        rows = blocks_ref.at[0, 0, pl.ds(0, count * chunk)]
        waiter(rows, block_send.at[lane], block_recv.at[0]).wait_send()

    def arrive(flow, part, at_line, at_row):
        rows = blocks_ref.at[at_line, at_row, pl.ds(part * chunk, chunk)]
        waiter(rows, block_send.at[0], block_recv.at[flow + part]).wait_recv()

    def arrived(flow, at_line, at_row):
        waiter(
            blocks_ref.at[at_line, at_row], block_send.at[0], block_recv.at[flow]
        ).wait_recv()

    def detour_out(part):
        rows = pl.ds(part * chunk, chunk)
        pltpu.make_async_remote_copy(
            src_ref=blocks_ref.at[line, row, rows],
            dst_ref=detour_ref.at[rows],
            send_sem=block_send.at[0],
            recv_sem=detour_recv.at[part],
            device_id=other_plane(row),
            device_id_type=pl.DeviceIdType.MESH,
        ).start()

    def detour_on(part):
        rows = pl.ds(part * chunk, chunk)
        waiter(detour_ref.at[rows], block_send.at[0], detour_recv.at[part]).wait_recv()
        pltpu.make_async_remote_copy(
            src_ref=detour_ref.at[rows],
            dst_ref=blocks_ref.at[line, hub - 1, rows],
            send_sem=block_send.at[3],
            recv_sem=block_recv.at[NEAR + part],
            device_id=other_plane(hub - 1),
            device_id_type=pl.DeviceIdType.MESH,
        ).start()

    def tell_ids(where):
        pltpu.make_async_remote_copy(
            src_ref=ids_ref.at[me],
            dst_ref=ids_ref.at[me],
            send_sem=ids_send,
            recv_sem=ids_recv,
            device_id=where,
            device_id_type=pl.DeviceIdType.MESH,
        ).start()

    def told_ids(count):
        waiter(ids_ref.at[pl.ds(0, count)], ids_send, ids_recv).wait_send()

    def hear_ids(count):
        waiter(ids_ref.at[pl.ds(0, count)], ids_send, ids_recv).wait_recv()

    def give(at_row, at_col, at_core, best):
        at = spot(at_col * CORES + at_core, at_row)
        given_ref[at] = best
        pltpu.make_async_remote_copy(
            src_ref=given_ref.at[at],
            dst_ref=taken_ref.at[me],
            send_sem=best_send,
            recv_sem=best_recv,
            device_id=device(at_row, at_col, at_core),
            device_id_type=pl.DeviceIdType.MESH,
        ).start()

    def gave(count):
        waiter(given_ref.at[pl.ds(0, count)], best_send, best_recv).wait_send()

    def take(*places):
        with jax.named_scope("w_back"):
            waiter(given_ref.at[pl.ds(0, len(places))], best_send, best_recv).wait_recv()
        best = taken_ref[spot(places[0][0], places[0][1])]
        for at_line, at_row in places[1:]:
            best = jnp.maximum(best, taken_ref[spot(at_line, at_row)])
        return best

    def finish(best):
        out_ref[...] = jnp.where(best > SAME / 2, jnp.maximum(best - SAME, -1.0), -1.0)

    def mark(at_line, at_row):
        shape = (row_count, row_count)
        down = jnp.transpose(jnp.broadcast_to(ids_ref[spot(at_line, at_row)], shape))
        here = down == lax.broadcasted_iota(jnp.int32, shape, 1)
        marks_ref[at_line, at_row] = jnp.where(here, SAME**0.5, 0.0).astype(jnp.bfloat16)

    def flat(ref, *index):
        values = ref[index]
        return values.reshape(-1, values.shape[-1])

    def operand(*indices):
        return jnp.concatenate(
            [
                jnp.concatenate([flat(blocks_ref, *index), flat(marks_ref, *index)], axis=1)
                for index in indices
            ],
            axis=0,
        )

    def scores(left, right):
        return lax.dot_general(
            left, right, (((1,), (1,)), ((), ())), preferred_element_type=jnp.float32
        )

    def down_max(values):
        return jnp.max(values, axis=0, keepdims=True)

    def fold(values):
        folded = values[:, :row_count]
        for at in range(1, values.shape[1] // row_count):
            folded = jnp.maximum(folded, values[:, at * row_count : (at + 1) * row_count])
        return folded

    def turn_max(folded):
        return down_max(jnp.transpose(folded))

    def without_self(values, start):
        down = lax.broadcasted_iota(jnp.int32, values.shape, 0)
        return jnp.where(
            down == lax.broadcasted_iota(jnp.int32, values.shape, 1) + start, -1.0, values
        )

    chip = pl.ds(col * CORES, CORES)

    def split(values):
        low, high = values[:, :row_count], values[:, row_count:]
        return jnp.where(core == 0, low, high), jnp.where(core == 0, high, low)

    def own_best():
        return down_max(
            without_self(scores(operand((chip, row)), operand((line, row))), core * row_count)
        )

    with jax.named_scope('e_small'):
        for copy in small_copies:
            copy.wait()
    counts = jnp.transpose(
        jnp.broadcast_to(lengths_ref[...].astype(jnp.float32), (row_count, row_count))
    )[:, 0:1]
    with jax.named_scope('e_states'):
        states_copy.wait()
    states = states_ref[...]
    summed = states[:, 0, :].astype(jnp.float32)
    for position in range(1, seq_len):
        token = states[:, position, :].astype(jnp.float32)
        summed = summed + jnp.where(counts > position, token, 0.0)
    pooled = (summed / counts).astype(jnp.bfloat16)
    projected = bias_ref[...]
    for at, copy in enumerate(weight_copies):
        with jax.named_scope('e_weight%d' % at):
            copy.wait()
        depth_at = slice(at * slab, (at + 1) * slab)
        projected = projected + jnp.dot(
            pooled[:, depth_at], weight_ref[depth_at], preferred_element_type=jnp.float32
        )
    hidden = jnp.tanh(projected)
    factor = lax.rsqrt(jnp.sum(hidden * hidden, axis=1, keepdims=True) + 1e-06)
    blocks_ref[line, row] = (hidden * factor).astype(jnp.bfloat16)

    with jax.named_scope("w_barrier"):
        pl.semaphore_wait(barrier, greetings)

    each_to(tell_ids)

    flow = jnp.where(row == 0, END, jnp.where(row == 1, NEAR, OUTER))
    for part in range(CHUNKS):
        if part < CHUNKS - ROUND:
            detours = (row == 1) & (core == 1)
        else:
            detours = (row == 1) & around

        @pl.when((row != hub) & jnp.logical_not(detours))
        def _():
            rows = blocks_ref.at[line, row, pl.ds(part * chunk, chunk)]
            pltpu.make_async_remote_copy(
                src_ref=rows,
                dst_ref=rows,
                send_sem=block_send.at[0],
                recv_sem=block_recv.at[flow + part],
                device_id=device(hub, col, core),
                device_id_type=pl.DeviceIdType.MESH,
            ).start()

        @pl.when(detours)
        def _():
            detour_out(part)

    for part in range(CHUNKS):
        send(SIBLING, part, line, row, sibling_device, 4)

    def send_across():
        for part in range(CHUNKS):
            send(ACROSS, part, line, row, device(row, far_col, core), 4)

    later = (row > hub) & (core == 1)

    @pl.when(jnp.logical_not(later))
    def _():
        send_across()

    mark(line, row)

    @pl.when(later)
    def _():
        sent(0, 1)
        send_across()

    @pl.when(row != hub)
    def _():
        for part in range(CHUNKS):
            arrive(ACROSS, part, across_line, row)

            @pl.when(row == 1)
            def _():
                send(AFTER, part, across_line, row, device(0, col, core), 1)

            if part < KEPT:

                @pl.when((row > hub) & (core == 0))
                def _():
                    send(CORNER, part, across_line, row, device(hub, col, core), 1)

        arrived(SIBLING, sibling_line, row)

        @pl.when(row > 0)
        def _():
            hear_ids(2)

        @pl.when(row == 0)
        def _():
            hear_ids(3)

        mark(across_line, row)
        mark(sibling_line, row)
        both = operand((chip, row))
        mine, other = split(down_max(scores(operand((across_line, row)), both)))
        best_ref[0:1] = jnp.maximum(mine, own_best())
        best_ref[1:2] = other

        @pl.when(row == 0)
        def _():
            with jax.named_scope("w_after"):
                arrived(AFTER, across_line, 1)
            mark(across_line, 1)
            after = scores(operand((across_line, 1)), operand((chip, row)))
            give(1, far_col, core, turn_max(fold(after)))
            mine, other = split(down_max(after))
            best_ref[0:1] = jnp.maximum(best_ref[0:1], mine)
            best_ref[1:2] = jnp.maximum(best_ref[1:2], other)

        give(row, col, far_core, best_ref[1:2])
        sent(4, 2)

        @pl.when(jnp.logical_not(later))
        def _():
            sent(0, 1)

        hubs = tuple((col * CORES + at_core, hub) for at_core in range(CORES))

        @pl.when(row == 0)
        def _():
            told_ids(4)
            gave(2)
            finish(jnp.maximum(best_ref[0:1], take((sibling_line, row), *hubs)))

        @pl.when(row == 1)
        def _():
            told_ids(5)
            gave(1)
            sent(1, 1)
            finish(
                jnp.maximum(best_ref[0:1], take((sibling_line, row), (across_line, 0), *hubs))
            )

        @pl.when(row > hub)
        def _():
            told_ids(5)
            gave(1)

            @pl.when(core == 0)
            def _():
                sent_parts(1, KEPT)

            finish(
                jnp.maximum(best_ref[0:1], take((sibling_line, row), (across_line, hub), *hubs))
            )

    @pl.when(row == hub)
    def _():
        outer, beside, corner = (line, hub + 1), (across_line, hub), (across_line, hub + 1)
        near, end = (line, hub - 1), (line, 0)
        near_too, end_too, outer_too = [(sibling_line, at) for at in (hub - 1, 0, hub + 1)]
        beside_too = (far_col * CORES + far_core, hub)
        far_chip = pl.ds(far_col * CORES, CORES)
        width = CORES * row_count

        def detour(part):
            passes = passing if part >= CHUNKS - ROUND else core == 1

            @pl.when(passes)
            def _():
                detour_on(part)

        def pass_outer(part):
            arrive(OUTER, part, *outer)
            send(OUTER_TOO, part, *outer, sibling_device, 1)

            @pl.when(True if part >= KEPT else core == 1)
            def _():
                send(CORNER, part, *outer, device(hub, far_col, core), 2)

        def pass_near(part):
            arrive(NEAR, part, *near)
            send(NEAR_TOO, part, *near, sibling_device, 1)

        def pass_end(part):
            arrive(END, part, *end)
            send(END_TOO, part, *end, sibling_device, 1)

        def pick(values, at):
            low, high = [
                values[:, (2 * at_core + at) * row_count : (2 * at_core + at + 1) * row_count]
                for at_core in range(CORES)
            ]
            return jnp.where(core == 0, low, high), jnp.where(core == 0, high, low)

        with jax.named_scope("w_a"):
            for part in range(2):
                detour(part)
                pass_outer(part)
                pass_end(part)
        with jax.named_scope("w_ids"):
            hear_ids(10)
        for at_row in range(ROWS):
            mark(sibling_line, at_row)
        for place in (outer, near, end, beside, beside_too, corner):
            mark(*place)
        with jax.named_scope("w_b"):
            for part in range(2, CHUNKS):
                detour(part)
                pass_outer(part)
                pass_end(part)
        arrived(SIBLING, sibling_line, hub)
        with jax.named_scope("w_beside"):
            for part in range(CHUNKS):
                arrive(ACROSS, part, *beside)
                send(BESIDE_TOO, part, *beside, sibling_device, 1)
        left_size = 2 * row_count
        hubs = operand((chip, hub))
        early = scores(operand((line, hub), outer), hubs)
        early_too = scores(operand(beside, end), hubs)
        own = without_self(early[:row_count], -core * row_count)
        hub_best = jnp.maximum(
            jnp.maximum(down_max(own), down_max(early[row_count:])), down_max(early_too)
        )
        early_folded = jnp.concatenate([fold(early[row_count:]), fold(early_too)], axis=0)
        outer_early, beside_early, end_early = [
            turn_max(early_folded[at * row_count : (at + 1) * row_count]) for at in range(3)
        ]
        with jax.named_scope("w_near"):
            for part in range(CHUNKS):
                pass_near(part)
        with jax.named_scope("w_too"):
            arrived(OUTER_TOO, *outer_too)
            arrived(BESIDE_TOO, *beside_too)
            arrived(END_TOO, *end_too)
        outer_scores = scores(operand(end, near, beside), operand((chip, hub + 1)))
        beside_scores = scores(operand(end, near), operand((far_chip, hub)))
        end_scores = scores(operand(near), operand((chip, 0)))
        mine, other = split(down_max(outer_scores))
        give(hub + 1, col, far_core, other)
        give(hub + 1, col, core, jnp.maximum(outer_early, mine))
        folded_ref[:left_size] = jnp.maximum(fold(outer_scores[:left_size]), fold(beside_scores))
        folded_ref[row_count:left_size] = jnp.maximum(
            folded_ref[row_count:left_size], fold(end_scores)
        )
        folded_ref[left_size:] = fold(outer_scores[left_size:])
        end_low = down_max(end_scores)
        beside_best = down_max(beside_scores)
        with jax.named_scope("w_corner"):
            arrived(CORNER, *corner)
        corner_end = scores(operand(corner), operand((chip, 0)))
        mine, other = split(jnp.maximum(end_low, down_max(corner_end)))
        give(0, col, far_core, other)
        end_best = jnp.maximum(end_early, turn_max(folded_ref[:row_count]))
        give(0, col, core, jnp.maximum(end_best, mine))
        with jax.named_scope("w_near_too"):
            arrived(NEAR_TOO, *near_too)
        corner_near = scores(operand(corner), operand((chip, hub - 1)))
        give(hub + 1, far_col, core, turn_max(jnp.maximum(fold(corner_end), fold(corner_near))))
        near_mine, near_other = split(down_max(corner_near))
        give(hub - 1, col, far_core, near_other)
        hub_scores = scores(operand(near), operand((chip, hub)))
        near_best = turn_max(jnp.maximum(folded_ref[row_count:left_size], fold(hub_scores)))
        give(hub - 1, col, core, jnp.maximum(near_best, near_mine))
        mine, other = split(beside_best)
        give(hub, far_col, far_core, other)
        beside_turned = jnp.maximum(beside_early, turn_max(folded_ref[left_size:]))
        give(hub, far_col, core, jnp.maximum(beside_turned, mine))
        hub_mine, hub_other = split(jnp.maximum(hub_best, down_max(hub_scores)))
        give(hub, col, far_core, hub_other)
        best_ref[0:1] = hub_mine
        with jax.named_scope("w_sent"):
            pass
        sent(4, 2)
        sent(1, 4)

        @pl.when(core == 1)
        def _():
            sent(2, 1)
            sent(3, 1)

        @pl.when(core == 0)
        def _():
            pass

        @pl.when((core == 0) & passing)
        def _():
            sent_parts(3, ROUND)

        told_ids(3)
        gave(10)
        finish(jnp.maximum(best_ref[0:1], take((sibling_line, hub), (across_line, hub), beside_too)))


def meet_body(token_states, lengths, cluster_id, proj_weight, proj_bias):
    row_count, seq_len, feat_dim = token_states.shape
    lines = lax.axis_size("docs") // ROWS * CORES
    vmem = pl.BlockSpec(memory_space=pltpu.VMEM)
    hbm = pl.BlockSpec(memory_space=pl.ANY)
    result = pl.pallas_call(
        meet_kernel,
        out_shape=pltpu.VMEM((1, row_count), jnp.float32),
        in_specs=[hbm] * 5,
        out_specs=vmem,
        scratch_shapes=[
            pltpu.VMEM((1, row_count), jnp.int32),
            pltpu.VMEM((1, feat_dim), jnp.float32),
            pltpu.VMEM(token_states.shape, jnp.bfloat16),
            pltpu.VMEM(proj_weight.shape, jnp.bfloat16),
            pltpu.VMEM((lines * ROWS, 1, row_count), jnp.int32),
            pltpu.VMEM((lines, ROWS, row_count, feat_dim), jnp.bfloat16),
            pltpu.VMEM((lines, ROWS, row_count, row_count), jnp.bfloat16),
            pltpu.VMEM((row_count, feat_dim), jnp.bfloat16),
            pltpu.VMEM((2, row_count), jnp.float32),
            pltpu.VMEM((3 * row_count, row_count), jnp.float32),
            pltpu.VMEM((lines * ROWS, 1, row_count), jnp.float32),
            pltpu.VMEM((lines * ROWS, 1, row_count), jnp.float32),
            pltpu.SemaphoreType.DMA((3,)),
            pltpu.SemaphoreType.DMA,
            pltpu.SemaphoreType.DMA((SLABS,)),
            pltpu.SemaphoreType.DMA((5,)),
            pltpu.SemaphoreType.DMA((FLOWS,)),
            pltpu.SemaphoreType.DMA((CHUNKS,)),
            pltpu.SemaphoreType.DMA,
            pltpu.SemaphoreType.DMA,
            pltpu.SemaphoreType.DMA,
            pltpu.SemaphoreType.DMA,
        ],
        compiler_params=pltpu.CompilerParams(collective_id=0, has_side_effects=True),
        name="scores",
    )(token_states, lengths[None, :], cluster_id[None, :], proj_weight, proj_bias[None, :])
    return result.reshape(row_count)

def solution(mesh):
    in_specs = (
        P(("groups", "docs", "help"), None, None),
        P(("groups", "docs", "help")),
        P(("groups", "docs", "help")),
        P(),
        P(),
    )
    out_specs = P(("groups", "docs", "help"))
    meets = mesh.shape["docs"] == 2 * ROWS and mesh.shape["help"] == CORES and mesh.shape["groups"] == 2
    return jax.shard_map(meet_body if meets else body, mesh=mesh, in_specs=in_specs, out_specs=out_specs, check_vma=False)
```

```python
import jax
import jax.numpy as jnp
from jax import lax
from jax.experimental import pallas as pl
from jax.experimental.pallas import tpu as pltpu
from jax.sharding import PartitionSpec as P

CL_OWN = 1


def partner(value, axis, bit):
    return lax.ppermute(value, axis, [(i, i ^ 1 << bit) for i in range(lax.axis_size(axis))])


def slot_maxima(own_emb, own_ids, self_pos, col_emb, col_ids):
    row_total = own_emb.shape[0]
    block = min(row_total, 512)
    col_pos = lax.broadcasted_iota(jnp.int32, (col_emb.shape[0],), 0)

    def block_max(pieces):
        part_emb, part_ids, part_self = pieces
        duplicate_scores = jnp.einsum(
            "rd,cd->rc", part_emb, col_emb, preferred_element_type=jnp.float32
        )
        match = (
            (part_ids[:, None] == col_ids[None, :])
            & (col_ids[None, :] >= 0)
            & (part_self[:, None] != col_pos[None, :])
        )
        return jnp.max(jnp.where(match, duplicate_scores, -1.0), axis=1)

    steps_count = row_total // block
    result = lax.map(
        block_max,
        (
            own_emb.reshape(steps_count, block, own_emb.shape[1]),
            own_ids.reshape(steps_count, block),
            self_pos.reshape(steps_count, block),
        ),
    )
    return result.reshape(row_total)


def body(token_states, lengths, cluster_id, proj_weight, proj_bias):
    row_count, seq_len, feat_dim = token_states.shape
    owners = lax.axis_size("docs")
    slot_cap = 2 * row_count // owners
    position_count = owners * slot_cap
    token_mask = (
        lax.broadcasted_iota(jnp.int32, (row_count, seq_len), 1) < lengths[:, None]
    ).astype(jnp.bfloat16)
    summed = jnp.einsum("rsd,rs->rd", token_states, token_mask, preferred_element_type=jnp.float32)
    pooled = (summed / lengths[:, None].astype(jnp.float32)).astype(jnp.bfloat16)
    hidden = jnp.tanh(jnp.dot(pooled, proj_weight, preferred_element_type=jnp.float32) + proj_bias)
    factor = lax.rsqrt(jnp.sum(hidden * hidden, axis=1, keepdims=True) + 1e-06)
    embedded = (hidden * factor).astype(jnp.bfloat16)
    dest_owner = cluster_id // CL_OWN
    same_owner = dest_owner[:, None] == dest_owner[None, :]
    earlier = lax.broadcasted_iota(jnp.int32, (row_count, row_count), 1) < lax.broadcasted_iota(
        jnp.int32, (row_count, row_count), 0
    )
    slot_rank = jnp.sum((same_owner & earlier).astype(jnp.int32), axis=1)
    target = dest_owner * slot_cap + slot_rank
    chooser = lax.broadcasted_iota(jnp.int32, (position_count, row_count), 0) == target[None, :]
    packed = jnp.dot(
        chooser.astype(jnp.bfloat16), embedded, preferred_element_type=jnp.float32
    ).astype(jnp.bfloat16)
    packed_ids = jnp.max(jnp.where(chooser, cluster_id[None, :], -1), axis=1)
    own_emb, own_ids = (
        lax.all_to_all(packed, "docs", split_axis=0, concat_axis=0, tiled=True),
        lax.all_to_all(packed_ids, "docs", split_axis=0, concat_axis=0, tiled=True),
    )
    mate_emb, mate_ids = partner((own_emb, own_ids), "help", 0)
    col_emb = jnp.concatenate([own_emb, mate_emb], axis=0)
    col_ids = jnp.concatenate([own_ids, mate_ids], axis=0)
    self_pos = lax.broadcasted_iota(jnp.int32, (position_count,), 0)
    maxima = slot_maxima(own_emb, own_ids, self_pos, col_emb, col_ids)
    returned = lax.all_to_all(maxima, "docs", split_axis=0, concat_axis=0, tiled=True)
    return jnp.max(jnp.where(chooser, returned[:, None], -3.0), axis=0)


ROWS = 4
CORES = 2
CHUNKS = 4
SLABS = 2
KEPT = 4
ROUND = 1
SAME = 4.0
SIBLING, CORNER, NEAR_TOO, END_TOO, OUTER_TOO, BESIDE_TOO, CORNER_TOO, AFTER = range(8)
ACROSS, OUTER, NEAR, END = (AFTER + 1 + CHUNKS * at for at in range(4))
FLOWS = END + CHUNKS


def meet_kernel(
    states_hbm,
    lengths_hbm,
    ids_hbm,
    weight_hbm,
    bias_hbm,
    out_ref,
    lengths_ref,
    bias_ref,
    states_ref,
    weight_ref,
    ids_ref,
    blocks_ref,
    marks_ref,
    detour_ref,
    best_ref,
    folded_ref,
    given_ref,
    taken_ref,
    small_sem,
    states_sem,
    weight_sem,
    block_send,
    block_recv,
    detour_recv,
    ids_send,
    ids_recv,
    best_send,
    best_recv,
):
    row_count, seq_len, feat_dim = states_ref.shape
    lines = blocks_ref.shape[0]
    columns = lines // CORES
    chunk = row_count // CHUNKS
    hub = ROWS - 2
    group = lax.axis_index("groups")
    docs = lax.axis_index("docs")
    core = lax.axis_index("help")
    depth = docs // columns
    col = docs % columns
    row = depth + group * (ROWS - 1 - 2 * depth)
    far_col = columns - 1 - col
    far_core = CORES - 1 - core
    line = col * CORES + core
    sibling_line = col * CORES + far_core
    across_line = far_col * CORES + core

    def device(at_row, at_col, at_core):
        at_depth = at_row + group * (ROWS - 1 - 2 * at_row)
        return {"docs": at_depth * columns + at_col, "help": at_core}

    def other_plane(at_row):
        at_depth = at_row + group * (ROWS - 1 - 2 * at_row)
        return {"groups": 1 - group, "docs": at_depth * columns + col, "help": core}

    def spot(at_line, at_row):
        return at_line * ROWS + at_row

    me = spot(line, row)
    sibling_device = device(row, col, far_core)

    states_copy = pltpu.make_async_copy(states_hbm, states_ref, states_sem)
    states_copy.start()
    small_copies = [
        pltpu.make_async_copy(source, held, small_sem.at[position])
        for position, (source, held) in enumerate(
            [(lengths_hbm, lengths_ref), (ids_hbm, ids_ref.at[me]), (bias_hbm, bias_ref)]
        )
    ]
    for copy in small_copies:
        copy.start()
    slab = feat_dim // SLABS
    weight_copies = [
        pltpu.make_async_copy(
            weight_hbm.at[pl.ds(at * slab, slab)],
            weight_ref.at[pl.ds(at * slab, slab)],
            weight_sem.at[at],
        )
        for at in range(SLABS)
    ]

    barrier = pltpu.get_barrier_semaphore()

    def greet(*wheres):
        for where in wheres:
            pl.semaphore_signal(
                barrier, inc=1, device_id=where, device_id_type=pl.DeviceIdType.MESH
            )

    around = (core == 1) | (group == 1)
    passing = (core == 1) | (group == 0)

    def each_to(act):
        @pl.when(row != hub)
        def _():
            for at_core in range(CORES):
                act(device(hub, col, at_core))

        @pl.when(row == 1)
        def _():
            act(device(0, far_col, core))

        @pl.when(row == hub)
        def _():
            act(device(hub, far_col, far_core))

        @pl.when(row > hub)
        def _():
            for at_core in range(CORES):
                act(device(hub, far_col, at_core))

        act(device(row, far_col, core))
        act(sibling_device)

    each_to(lambda where: greet(where))

    @pl.when(row == 0)
    def _():
        greet(device(1, col, core), device(1, far_col, core))

    @pl.when(row == 1)
    def _():
        greet(device(0, col, core))

    @pl.when(row == hub)
    def _():
        for at_core in range(CORES):
            for at_row in (0, 1, hub + 1):
                greet(device(at_row, col, at_core))
            greet(device(hub + 1, far_col, at_core))

    @pl.when((row == 1) & around)
    def _():
        greet(other_plane(row))

    @pl.when((row == hub) & passing)
    def _():
        greet(other_plane(row), other_plane(hub - 1))

    @pl.when((row == hub) & around & jnp.logical_not((core == 1) & passing))
    def _():
        greet(other_plane(hub - 1))

    for copy in weight_copies:
        copy.start()

    greetings = (
        2
        + 4 * (row < hub)
        + 9 * (row == hub)
        + 4 * (row > hub)
        + ((row == 1) & around)
        + (row == hub) * (1 + passing)
    )

    def send(flow, part, at_line, at_row, where, lane=0):
        rows = blocks_ref.at[at_line, at_row, pl.ds(part * chunk, chunk)]
        pltpu.make_async_remote_copy(
            src_ref=rows,
            dst_ref=rows,
            send_sem=block_send.at[lane],
            recv_sem=block_recv.at[flow if flow <= AFTER else flow + part],
            device_id=where,
            device_id_type=pl.DeviceIdType.MESH,
        ).start()

    def waiter(held, send_sem, recv_sem):
        return pltpu.make_async_remote_copy(
            src_ref=held,
            dst_ref=held,
            send_sem=send_sem,
            recv_sem=recv_sem,
            device_id=sibling_device,
            device_id_type=pl.DeviceIdType.MESH,
        )

    def sent(lane, count):
        waiter(
            blocks_ref.at[0, pl.ds(0, count)], block_send.at[lane], block_recv.at[0]
        ).wait_send()

    def sent_parts(lane, count):
        rows = blocks_ref.at[0, 0, pl.ds(0, count * chunk)]
        waiter(rows, block_send.at[lane], block_recv.at[0]).wait_send()

    def arrive(flow, part, at_line, at_row):
        rows = blocks_ref.at[at_line, at_row, pl.ds(part * chunk, chunk)]
        waiter(rows, block_send.at[0], block_recv.at[flow + part]).wait_recv()

    def arrived(flow, at_line, at_row):
        waiter(
            blocks_ref.at[at_line, at_row], block_send.at[0], block_recv.at[flow]
        ).wait_recv()

    def detour_out(part):
        rows = pl.ds(part * chunk, chunk)
        pltpu.make_async_remote_copy(
            src_ref=blocks_ref.at[line, row, rows],
            dst_ref=detour_ref.at[rows],
            send_sem=block_send.at[0],
            recv_sem=detour_recv.at[part],
            device_id=other_plane(row),
            device_id_type=pl.DeviceIdType.MESH,
        ).start()

    def detour_on(part):
        rows = pl.ds(part * chunk, chunk)
        waiter(detour_ref.at[rows], block_send.at[0], detour_recv.at[part]).wait_recv()
        pltpu.make_async_remote_copy(
            src_ref=detour_ref.at[rows],
            dst_ref=blocks_ref.at[line, hub - 1, rows],
            send_sem=block_send.at[3],
            recv_sem=block_recv.at[NEAR + part],
            device_id=other_plane(hub - 1),
            device_id_type=pl.DeviceIdType.MESH,
        ).start()

    def tell_ids(where):
        pltpu.make_async_remote_copy(
            src_ref=ids_ref.at[me],
            dst_ref=ids_ref.at[me],
            send_sem=ids_send,
            recv_sem=ids_recv,
            device_id=where,
            device_id_type=pl.DeviceIdType.MESH,
        ).start()

    def told_ids(count):
        waiter(ids_ref.at[pl.ds(0, count)], ids_send, ids_recv).wait_send()

    def hear_ids(count):
        waiter(ids_ref.at[pl.ds(0, count)], ids_send, ids_recv).wait_recv()

    def give(at_row, at_col, at_core, best):
        at = spot(at_col * CORES + at_core, at_row)
        given_ref[at] = best
        pltpu.make_async_remote_copy(
            src_ref=given_ref.at[at],
            dst_ref=taken_ref.at[me],
            send_sem=best_send,
            recv_sem=best_recv,
            device_id=device(at_row, at_col, at_core),
            device_id_type=pl.DeviceIdType.MESH,
        ).start()

    def gave(count):
        waiter(given_ref.at[pl.ds(0, count)], best_send, best_recv).wait_send()

    def take(*places):
        with jax.named_scope("w_back"):
            waiter(given_ref.at[pl.ds(0, len(places))], best_send, best_recv).wait_recv()
        best = taken_ref[spot(places[0][0], places[0][1])]
        for at_line, at_row in places[1:]:
            best = jnp.maximum(best, taken_ref[spot(at_line, at_row)])
        return best

    def finish(best):
        out_ref[...] = jnp.where(best > SAME / 2, jnp.maximum(best - SAME, -1.0), -1.0)

    def mark(at_line, at_row):
        shape = (row_count, row_count)
        down = jnp.transpose(jnp.broadcast_to(ids_ref[spot(at_line, at_row)], shape))
        here = down == lax.broadcasted_iota(jnp.int32, shape, 1)
        marks_ref[at_line, at_row] = jnp.where(here, SAME**0.5, 0.0).astype(jnp.bfloat16)

    def flat(ref, *index):
        values = ref[index]
        return values.reshape(-1, values.shape[-1])

    def operand(*indices):
        return jnp.concatenate(
            [
                jnp.concatenate([flat(blocks_ref, *index), flat(marks_ref, *index)], axis=1)
                for index in indices
            ],
            axis=0,
        )

    def scores(left, right):
        return lax.dot_general(
            left, right, (((1,), (1,)), ((), ())), preferred_element_type=jnp.float32
        )

    def down_max(values):
        return jnp.max(values, axis=0, keepdims=True)

    def fold(values):
        folded = values[:, :row_count]
        for at in range(1, values.shape[1] // row_count):
            folded = jnp.maximum(folded, values[:, at * row_count : (at + 1) * row_count])
        return folded

    def turn_max(folded):
        return down_max(jnp.transpose(folded))

    def without_self(values, start):
        down = lax.broadcasted_iota(jnp.int32, values.shape, 0)
        return jnp.where(
            down == lax.broadcasted_iota(jnp.int32, values.shape, 1) + start, -1.0, values
        )

    chip = pl.ds(col * CORES, CORES)

    def split(values):
        low, high = values[:, :row_count], values[:, row_count:]
        return jnp.where(core == 0, low, high), jnp.where(core == 0, high, low)

    def own_best():
        return down_max(
            without_self(scores(operand((chip, row)), operand((line, row))), core * row_count)
        )

    with jax.named_scope('e_small'):
        for copy in small_copies:
            copy.wait()
    counts = jnp.transpose(
        jnp.broadcast_to(lengths_ref[...].astype(jnp.float32), (row_count, row_count))
    )[:, 0:1]
    with jax.named_scope('e_states'):
        states_copy.wait()
    states = states_ref[...]
    summed = states[:, 0, :].astype(jnp.float32)
    for position in range(1, seq_len):
        token = states[:, position, :].astype(jnp.float32)
        summed = summed + jnp.where(counts > position, token, 0.0)
    pooled = (summed / counts).astype(jnp.bfloat16)
    projected = bias_ref[...]
    for at, copy in enumerate(weight_copies):
        with jax.named_scope('e_weight%d' % at):
            copy.wait()
        depth_at = slice(at * slab, (at + 1) * slab)
        projected = projected + jnp.dot(
            pooled[:, depth_at], weight_ref[depth_at], preferred_element_type=jnp.float32
        )
    hidden = jnp.tanh(projected)
    factor = lax.rsqrt(jnp.sum(hidden * hidden, axis=1, keepdims=True) + 1e-06)
    blocks_ref[line, row] = (hidden * factor).astype(jnp.bfloat16)

    with jax.named_scope("w_barrier"):
        pl.semaphore_wait(barrier, greetings)

    each_to(tell_ids)

    flow = jnp.where(row == 0, END, jnp.where(row == 1, NEAR, OUTER))
    for part in range(CHUNKS):
        if part < CHUNKS - ROUND:
            detours = (row == 1) & (core == 1)
        else:
            detours = (row == 1) & around

        @pl.when((row != hub) & jnp.logical_not(detours))
        def _():
            rows = blocks_ref.at[line, row, pl.ds(part * chunk, chunk)]
            pltpu.make_async_remote_copy(
                src_ref=rows,
                dst_ref=rows,
                send_sem=block_send.at[0],
                recv_sem=block_recv.at[flow + part],
                device_id=device(hub, col, core),
                device_id_type=pl.DeviceIdType.MESH,
            ).start()

        @pl.when(detours)
        def _():
            detour_out(part)

    for part in range(CHUNKS):
        send(SIBLING, part, line, row, sibling_device, 4)

    def send_across():
        for part in range(CHUNKS):
            send(ACROSS, part, line, row, device(row, far_col, core), 4)

    later = (row > hub) & (core == 1)

    @pl.when(jnp.logical_not(later))
    def _():
        send_across()

    mark(line, row)

    @pl.when(later)
    def _():
        sent(0, 1)
        send_across()

    @pl.when(row != hub)
    def _():
        for part in range(CHUNKS):
            arrive(ACROSS, part, across_line, row)

            @pl.when(row == 1)
            def _():
                send(AFTER, part, across_line, row, device(0, col, core), 1)

            if part < KEPT:

                @pl.when((row > hub) & (core == 0))
                def _():
                    send(CORNER, part, across_line, row, device(hub, col, core), 1)

        arrived(SIBLING, sibling_line, row)

        @pl.when(row > 0)
        def _():
            hear_ids(2)

        @pl.when(row == 0)
        def _():
            hear_ids(3)

        mark(across_line, row)
        mark(sibling_line, row)
        both = operand((chip, row))
        mine, other = split(down_max(scores(operand((across_line, row)), both)))
        best_ref[0:1] = jnp.maximum(mine, own_best())
        best_ref[1:2] = other

        @pl.when(row == 0)
        def _():
            with jax.named_scope("w_after"):
                arrived(AFTER, across_line, 1)
            mark(across_line, 1)
            after = scores(operand((across_line, 1)), operand((chip, row)))
            give(1, far_col, core, turn_max(fold(after)))
            mine, other = split(down_max(after))
            best_ref[0:1] = jnp.maximum(best_ref[0:1], mine)
            best_ref[1:2] = jnp.maximum(best_ref[1:2], other)

        give(row, col, far_core, best_ref[1:2])
        sent(4, 2)

        @pl.when(jnp.logical_not(later))
        def _():
            sent(0, 1)

        hubs = tuple((col * CORES + at_core, hub) for at_core in range(CORES))

        @pl.when(row == 0)
        def _():
            told_ids(4)
            gave(2)
            finish(jnp.maximum(best_ref[0:1], take((sibling_line, row), *hubs)))

        @pl.when(row == 1)
        def _():
            told_ids(5)
            gave(1)
            sent(1, 1)

            @pl.when(group == 0)
            def _():
                best = take((sibling_line, row), (across_line, 0), *hubs)
                finish(jnp.maximum(best_ref[0:1], best))

            @pl.when(group == 1)
            def _():
                best = take((sibling_line, row), (across_line, 0), (line, hub))
                finish(jnp.maximum(best_ref[0:1], best))

        @pl.when(row > hub)
        def _():
            told_ids(6)
            gave(1)

            @pl.when(core == 0)
            def _():
                sent_parts(1, KEPT)

            @pl.when(group == 0)
            def _():
                best = take((sibling_line, row), (across_line, hub), *hubs)
                finish(jnp.maximum(best_ref[0:1], best))

            @pl.when(group == 1)
            def _():
                far_hub = (far_col * CORES + far_core, hub)
                best = take((sibling_line, row), (across_line, hub), far_hub, *hubs)
                finish(jnp.maximum(best_ref[0:1], best))

    @pl.when(row == hub)
    def _():
        outer, beside, corner = (line, hub + 1), (across_line, hub), (across_line, hub + 1)
        near, end = (line, hub - 1), (line, 0)
        near_too, end_too, outer_too = [(sibling_line, at) for at in (hub - 1, 0, hub + 1)]
        beside_too = (far_col * CORES + far_core, hub)
        corner_too = (far_col * CORES + far_core, hub + 1)
        forward = group == 0
        far_chip = pl.ds(far_col * CORES, CORES)
        width = CORES * row_count

        def detour(part):
            @pl.when(core == 1)
            def _():
                detour_on(part)

        def pass_outer(part):
            arrive(OUTER, part, *outer)
            send(OUTER_TOO, part, *outer, sibling_device, 1)

            @pl.when(True if part >= KEPT else core == 1)
            def _():
                send(CORNER, part, *outer, device(hub, far_col, core), 2)

        def pass_near(part):
            arrive(NEAR, part, *near)

            @pl.when(forward)
            def _():
                send(NEAR_TOO, part, *near, sibling_device, 1)

        def pass_end(part):
            arrive(END, part, *end)
            send(END_TOO, part, *end, sibling_device, 1)

        def pick(values, at):
            low, high = [
                values[:, (2 * at_core + at) * row_count : (2 * at_core + at + 1) * row_count]
                for at_core in range(CORES)
            ]
            return jnp.where(core == 0, low, high), jnp.where(core == 0, high, low)

        @pl.when((core == 0) & passing)
        def _():
            for part in range(CHUNKS - ROUND, CHUNKS):
                detour_on(part)

        with jax.named_scope("w_a"):
            for part in range(2):
                detour(part)
                pass_outer(part)
                pass_end(part)
        with jax.named_scope("w_ids"):
            hear_ids(11)
        for at_row in range(ROWS):
            mark(sibling_line, at_row)
        for place in (outer, near, end, beside, beside_too, corner, corner_too):
            mark(*place)
        with jax.named_scope("w_b"):
            for part in range(2, CHUNKS):
                detour(part)
                pass_outer(part)
                pass_end(part)
        arrived(SIBLING, sibling_line, hub)
        with jax.named_scope("w_beside"):
            for part in range(CHUNKS):
                arrive(ACROSS, part, *beside)
                send(BESIDE_TOO, part, *beside, sibling_device, 1)
        left_size = 2 * row_count
        hubs = operand((chip, hub))
        early = scores(operand((line, hub), outer), hubs)
        early_too = scores(operand(beside, end), hubs)
        own = without_self(early[:row_count], -core * row_count)
        hub_best = jnp.maximum(
            jnp.maximum(down_max(own), down_max(early[row_count:])), down_max(early_too)
        )
        outer_early = turn_max(fold(early[row_count:]))
        early_folded = fold(early_too)
        outers, besides, ends = (chip, hub + 1), (far_chip, hub), (chip, 0)
        with jax.named_scope("w_outer_too"):
            arrived(OUTER_TOO, *outer_too)
        beside_outer = scores(operand(beside), operand(outers))
        end_outer = scores(operand(end), operand(outers))
        outer_low = jnp.maximum(down_max(beside_outer), down_max(end_outer))
        beside_early = turn_max(jnp.maximum(early_folded[:row_count], fold(beside_outer)))
        end_early = turn_max(jnp.maximum(early_folded[row_count:], fold(end_outer)))

        def give_outers(near_outer):
            mine, other = split(jnp.maximum(outer_low, down_max(near_outer)))
            give(hub + 1, col, far_core, other)
            give(hub + 1, col, core, jnp.maximum(outer_early, mine))

        def give_ends(best, folded):
            mine, other = split(best)
            give(0, col, far_core, other)
            mine = jnp.maximum(jnp.maximum(end_early, mine), turn_max(folded))
            give(0, col, core, mine)

        def give_besides(best):
            mine, other = split(best)
            give(hub, far_col, far_core, other)
            give(hub, far_col, core, jnp.maximum(beside_early, mine))

        def give_hubs(hub_scores):
            mine, other = split(jnp.maximum(hub_best, down_max(hub_scores)))
            give(hub, col, far_core, other)
            best_ref[0:1] = mine

        @pl.when(group == 0)
        def _():
            with jax.named_scope("w_near"):
                for part in range(CHUNKS):
                    pass_near(part)
            with jax.named_scope("w_too"):
                arrived(BESIDE_TOO, *beside_too)
                arrived(END_TOO, *end_too)
            end_beside = scores(operand(end), operand(besides))
            near_end = scores(operand(near), operand(ends))
            with jax.named_scope("w_corner"):
                arrived(CORNER, *corner)
            corner_operand = operand(corner)
            corner_end = jnp.concatenate(
                [
                    scores(corner_operand, operand((col * CORES + at_core, 0)))
                    for at_core in range(CORES)
                ],
                axis=1,
            )
            give_ends(
                jnp.maximum(down_max(near_end), down_max(corner_end)), fold(end_beside)
            )
            near_outer = scores(operand(near), operand(outers))
            near_beside = scores(operand(near), operand(besides))
            give_outers(near_outer)
            near_folded = jnp.maximum(
                fold(near_end), jnp.maximum(fold(near_outer), fold(near_beside))
            )
            with jax.named_scope("w_near_too"):
                arrived(NEAR_TOO, *near_too)
            corner_near = scores(operand(corner), operand((chip, hub - 1)))
            hub_scores = scores(operand(near), hubs)
            give(
                hub + 1, far_col, core, turn_max(jnp.maximum(fold(corner_end), fold(corner_near)))
            )
            mine, other = split(down_max(corner_near))
            give(hub - 1, col, far_core, other)
            near_best = turn_max(jnp.maximum(near_folded, fold(hub_scores)))
            give(hub - 1, col, core, jnp.maximum(near_best, mine))
            give_besides(jnp.maximum(down_max(end_beside), down_max(near_beside)))
            give_hubs(hub_scores)

        @pl.when(group == 1)
        def _():
            with jax.named_scope("w_corner"):
                arrived(CORNER, *corner)
            for part in range(CHUNKS):
                send(CORNER_TOO, part, *corner, sibling_device, 1)
            for part in range(CHUNKS):
                with jax.named_scope("w_near%d" % part):
                    pass_near(part)
            with jax.named_scope("w_too"):
                arrived(BESIDE_TOO, *beside_too)
                arrived(END_TOO, *end_too)
                arrived(CORNER_TOO, *corner_too)
            left = operand(end, near)
            near_outer = scores(operand(near), operand(outers))
            left_corner = scores(left, operand((far_chip, hub + 1)))
            give_outers(near_outer)
            mine, other = split(down_max(left_corner))
            give(hub + 1, far_col, far_core, other)
            give(hub + 1, far_col, core, mine)
            left_beside = scores(left, operand(besides))
            near_end = scores(operand(near), operand(ends))
            left_folded = jnp.maximum(fold(left_corner), fold(left_beside))
            give_ends(down_max(near_end), left_folded[:row_count])
            hub_scores = scores(operand(near), hubs)
            near_folded = jnp.maximum(
                jnp.maximum(fold(near_end), fold(near_outer)),
                jnp.maximum(left_folded[row_count:], fold(hub_scores)),
            )
            give(hub - 1, col, core, turn_max(near_folded))
            give_besides(down_max(left_beside))
            give_hubs(hub_scores)

        sent(4, 2)
        sent(1, 4)

        @pl.when(core == 1)
        def _():
            sent(2, 1)
            sent(3, 1)

        @pl.when(core == 0)
        def _():
            pass

        @pl.when((core == 0) & passing)
        def _():
            sent_parts(3, ROUND)

        told_ids(3)
        gave(10)
        finish(jnp.maximum(best_ref[0:1], take((sibling_line, hub), (across_line, hub), beside_too)))


def meet_body(token_states, lengths, cluster_id, proj_weight, proj_bias):
    row_count, seq_len, feat_dim = token_states.shape
    lines = lax.axis_size("docs") // ROWS * CORES
    vmem = pl.BlockSpec(memory_space=pltpu.VMEM)
    hbm = pl.BlockSpec(memory_space=pl.ANY)
    result = pl.pallas_call(
        meet_kernel,
        out_shape=pltpu.VMEM((1, row_count), jnp.float32),
        in_specs=[hbm] * 5,
        out_specs=vmem,
        scratch_shapes=[
            pltpu.VMEM((1, row_count), jnp.int32),
            pltpu.VMEM((1, feat_dim), jnp.float32),
            pltpu.VMEM(token_states.shape, jnp.bfloat16),
            pltpu.VMEM(proj_weight.shape, jnp.bfloat16),
            pltpu.VMEM((lines * ROWS, 1, row_count), jnp.int32),
            pltpu.VMEM((lines, ROWS, row_count, feat_dim), jnp.bfloat16),
            pltpu.VMEM((lines, ROWS, row_count, row_count), jnp.bfloat16),
            pltpu.VMEM((row_count, feat_dim), jnp.bfloat16),
            pltpu.VMEM((2, row_count), jnp.float32),
            pltpu.VMEM((3 * row_count, row_count), jnp.float32),
            pltpu.VMEM((lines * ROWS, 1, row_count), jnp.float32),
            pltpu.VMEM((lines * ROWS, 1, row_count), jnp.float32),
            pltpu.SemaphoreType.DMA((3,)),
            pltpu.SemaphoreType.DMA,
            pltpu.SemaphoreType.DMA((SLABS,)),
            pltpu.SemaphoreType.DMA((5,)),
            pltpu.SemaphoreType.DMA((FLOWS,)),
            pltpu.SemaphoreType.DMA((CHUNKS,)),
            pltpu.SemaphoreType.DMA,
            pltpu.SemaphoreType.DMA,
            pltpu.SemaphoreType.DMA,
            pltpu.SemaphoreType.DMA,
        ],
        compiler_params=pltpu.CompilerParams(collective_id=0, has_side_effects=True),
        name="scores",
    )(token_states, lengths[None, :], cluster_id[None, :], proj_weight, proj_bias[None, :])
    return result.reshape(row_count)

def solution(mesh):
    in_specs = (
        P(("groups", "docs", "help"), None, None),
        P(("groups", "docs", "help")),
        P(("groups", "docs", "help")),
        P(),
        P(),
    )
    out_specs = P(("groups", "docs", "help"))
    meets = mesh.shape["docs"] == 2 * ROWS and mesh.shape["help"] == CORES and mesh.shape["groups"] == 2
    return jax.shard_map(meet_body if meets else body, mesh=mesh, in_specs=in_specs, out_specs=out_specs, check_vma=False)
```

```python
import jax
import jax.numpy as jnp
from jax import lax
from jax.experimental import pallas as pl
from jax.experimental.pallas import tpu as pltpu
from jax.sharding import PartitionSpec as P

CL_OWN = 1


def partner(value, axis, bit):
    return lax.ppermute(value, axis, [(i, i ^ 1 << bit) for i in range(lax.axis_size(axis))])


def slot_maxima(own_emb, own_ids, self_pos, col_emb, col_ids):
    row_total = own_emb.shape[0]
    block = min(row_total, 512)
    col_pos = lax.broadcasted_iota(jnp.int32, (col_emb.shape[0],), 0)

    def block_max(pieces):
        part_emb, part_ids, part_self = pieces
        duplicate_scores = jnp.einsum(
            "rd,cd->rc", part_emb, col_emb, preferred_element_type=jnp.float32
        )
        match = (
            (part_ids[:, None] == col_ids[None, :])
            & (col_ids[None, :] >= 0)
            & (part_self[:, None] != col_pos[None, :])
        )
        return jnp.max(jnp.where(match, duplicate_scores, -1.0), axis=1)

    steps_count = row_total // block
    result = lax.map(
        block_max,
        (
            own_emb.reshape(steps_count, block, own_emb.shape[1]),
            own_ids.reshape(steps_count, block),
            self_pos.reshape(steps_count, block),
        ),
    )
    return result.reshape(row_total)


def body(token_states, lengths, cluster_id, proj_weight, proj_bias):
    row_count, seq_len, feat_dim = token_states.shape
    owners = lax.axis_size("docs")
    slot_cap = 2 * row_count // owners
    position_count = owners * slot_cap
    token_mask = (
        lax.broadcasted_iota(jnp.int32, (row_count, seq_len), 1) < lengths[:, None]
    ).astype(jnp.bfloat16)
    summed = jnp.einsum("rsd,rs->rd", token_states, token_mask, preferred_element_type=jnp.float32)
    pooled = (summed / lengths[:, None].astype(jnp.float32)).astype(jnp.bfloat16)
    hidden = jnp.tanh(jnp.dot(pooled, proj_weight, preferred_element_type=jnp.float32) + proj_bias)
    factor = lax.rsqrt(jnp.sum(hidden * hidden, axis=1, keepdims=True) + 1e-06)
    embedded = (hidden * factor).astype(jnp.bfloat16)
    dest_owner = cluster_id // CL_OWN
    same_owner = dest_owner[:, None] == dest_owner[None, :]
    earlier = lax.broadcasted_iota(jnp.int32, (row_count, row_count), 1) < lax.broadcasted_iota(
        jnp.int32, (row_count, row_count), 0
    )
    slot_rank = jnp.sum((same_owner & earlier).astype(jnp.int32), axis=1)
    target = dest_owner * slot_cap + slot_rank
    chooser = lax.broadcasted_iota(jnp.int32, (position_count, row_count), 0) == target[None, :]
    packed = jnp.dot(
        chooser.astype(jnp.bfloat16), embedded, preferred_element_type=jnp.float32
    ).astype(jnp.bfloat16)
    packed_ids = jnp.max(jnp.where(chooser, cluster_id[None, :], -1), axis=1)
    own_emb, own_ids = (
        lax.all_to_all(packed, "docs", split_axis=0, concat_axis=0, tiled=True),
        lax.all_to_all(packed_ids, "docs", split_axis=0, concat_axis=0, tiled=True),
    )
    mate_emb, mate_ids = partner((own_emb, own_ids), "help", 0)
    col_emb = jnp.concatenate([own_emb, mate_emb], axis=0)
    col_ids = jnp.concatenate([own_ids, mate_ids], axis=0)
    self_pos = lax.broadcasted_iota(jnp.int32, (position_count,), 0)
    maxima = slot_maxima(own_emb, own_ids, self_pos, col_emb, col_ids)
    returned = lax.all_to_all(maxima, "docs", split_axis=0, concat_axis=0, tiled=True)
    return jnp.max(jnp.where(chooser, returned[:, None], -3.0), axis=0)


ROWS = 4
CORES = 2
CHUNKS = 4
SLABS = 2
KEPT = 4
ROUND = 1
SAME = 4.0
SIBLING, CORNER, NEAR_TOO, END_TOO, OUTER_TOO, BESIDE_TOO = range(6)
AFTER, CORNER_TOO, WHOLE = CORNER, NEAR_TOO, BESIDE_TOO
ACROSS, OUTER, NEAR, END = (WHOLE + 1 + CHUNKS * at for at in range(4))
FLOWS = END + CHUNKS


def meet_kernel(
    states_hbm,
    lengths_hbm,
    ids_hbm,
    weight_hbm,
    bias_hbm,
    out_ref,
    lengths_ref,
    bias_ref,
    states_ref,
    weight_ref,
    ids_ref,
    blocks_ref,
    marks_ref,
    detour_ref,
    best_ref,
    given_ref,
    taken_ref,
    block_send,
    block_recv,
    detour_recv,
    ids_send,
    ids_recv,
    best_send,
    best_recv,
):
    row_count, seq_len, feat_dim = states_ref.shape
    lines = blocks_ref.shape[0]
    columns = lines // CORES
    chunk = row_count // CHUNKS
    hub = ROWS - 2
    group = lax.axis_index("groups")
    docs = lax.axis_index("docs")
    core = lax.axis_index("help")
    depth = docs // columns
    col = docs % columns
    row = depth + group * (ROWS - 1 - 2 * depth)
    far_col = columns - 1 - col
    far_core = CORES - 1 - core
    line = col * CORES + core
    sibling_line = col * CORES + far_core
    across_line = far_col * CORES + core

    def device(at_row, at_col, at_core):
        at_depth = at_row + group * (ROWS - 1 - 2 * at_row)
        return {"docs": at_depth * columns + at_col, "help": at_core}

    def other_plane(at_row):
        at_depth = at_row + group * (ROWS - 1 - 2 * at_row)
        return {"groups": 1 - group, "docs": at_depth * columns + col, "help": core}

    def spot(at_line, at_row):
        return at_line * ROWS + at_row

    me = spot(line, row)
    sibling_device = device(row, col, far_core)

    states_copy = pltpu.make_async_copy(states_hbm, states_ref, block_send.at[3])
    states_copy.start()
    small_copies = [
        pltpu.make_async_copy(source, held, block_send.at[position])
        for position, (source, held) in enumerate(
            [(lengths_hbm, lengths_ref), (ids_hbm, ids_ref.at[me]), (bias_hbm, bias_ref)]
        )
    ]
    for copy in small_copies:
        copy.start()
    slab = feat_dim // SLABS
    weight_copies = [
        pltpu.make_async_copy(
            weight_hbm.at[pl.ds(at * slab, slab)],
            weight_ref.at[pl.ds(at * slab, slab)],
            best_send if at else block_send.at[4],
        )
        for at in range(SLABS)
    ]

    barrier = pltpu.get_barrier_semaphore()

    def greet(*wheres):
        for where in wheres:
            pl.semaphore_signal(
                barrier, inc=1, device_id=where, device_id_type=pl.DeviceIdType.MESH
            )

    around = (core == 1) | (group == 1)
    passing = (core == 1) | (group == 0)

    def each_to(act):
        @pl.when(row != hub)
        def _():
            for at_core in range(CORES):
                act(device(hub, col, at_core))

        @pl.when(row == 1)
        def _():
            act(device(0, far_col, core))

        @pl.when(row == hub)
        def _():
            act(device(hub, far_col, far_core))

        @pl.when(row > hub)
        def _():
            for at_core in range(CORES):
                act(device(hub, far_col, at_core))

        act(device(row, far_col, core))
        act(sibling_device)

    each_to(lambda where: greet(where))

    @pl.when(row == 0)
    def _():
        greet(device(1, col, core), device(1, far_col, core))

    @pl.when(row == 1)
    def _():
        greet(device(0, col, core))

    @pl.when(row == hub)
    def _():
        for at_core in range(CORES):
            for at_row in (0, 1, hub + 1):
                greet(device(at_row, col, at_core))
            greet(device(hub + 1, far_col, at_core))

    @pl.when((row == 1) & around)
    def _():
        greet(other_plane(row))

    @pl.when((row == hub) & passing)
    def _():
        greet(other_plane(row), other_plane(hub - 1))

    @pl.when((row == hub) & around & jnp.logical_not((core == 1) & passing))
    def _():
        greet(other_plane(hub - 1))

    for copy in weight_copies:
        copy.start()

    greetings = (
        2
        + 4 * (row < hub)
        + 9 * (row == hub)
        + 4 * (row > hub)
        + ((row == 1) & around)
        + (row == hub) * (1 + passing)
    )

    def send(flow, part, at_line, at_row, where, lane=0):
        rows = blocks_ref.at[at_line, at_row, pl.ds(part * chunk, chunk)]
        pltpu.make_async_remote_copy(
            src_ref=rows,
            dst_ref=rows,
            send_sem=block_send.at[lane],
            recv_sem=block_recv.at[flow if flow <= WHOLE else flow + part],
            device_id=where,
            device_id_type=pl.DeviceIdType.MESH,
        ).start()

    def waiter(held, send_sem, recv_sem):
        return pltpu.make_async_remote_copy(
            src_ref=held,
            dst_ref=held,
            send_sem=send_sem,
            recv_sem=recv_sem,
            device_id=sibling_device,
            device_id_type=pl.DeviceIdType.MESH,
        )

    def sent(lane, count):
        waiter(
            blocks_ref.at[0, pl.ds(0, count)], block_send.at[lane], block_recv.at[0]
        ).wait_send()

    def sent_parts(lane, count):
        rows = blocks_ref.at[0, 0, pl.ds(0, count * chunk)]
        waiter(rows, block_send.at[lane], block_recv.at[0]).wait_send()

    def arrive(flow, part, at_line, at_row):
        rows = blocks_ref.at[at_line, at_row, pl.ds(part * chunk, chunk)]
        waiter(rows, block_send.at[0], block_recv.at[flow + part]).wait_recv()

    def arrived(flow, at_line, at_row):
        waiter(
            blocks_ref.at[at_line, at_row], block_send.at[0], block_recv.at[flow]
        ).wait_recv()

    def detour_out(part):
        rows = pl.ds(part * chunk, chunk)
        pltpu.make_async_remote_copy(
            src_ref=blocks_ref.at[line, row, rows],
            dst_ref=detour_ref.at[rows],
            send_sem=block_send.at[0],
            recv_sem=detour_recv.at[part],
            device_id=other_plane(row),
            device_id_type=pl.DeviceIdType.MESH,
        ).start()

    def detour_on(part):
        rows = pl.ds(part * chunk, chunk)
        waiter(detour_ref.at[rows], block_send.at[0], detour_recv.at[part]).wait_recv()
        pltpu.make_async_remote_copy(
            src_ref=detour_ref.at[rows],
            dst_ref=blocks_ref.at[line, hub - 1, rows],
            send_sem=block_send.at[3],
            recv_sem=block_recv.at[NEAR + part],
            device_id=other_plane(hub - 1),
            device_id_type=pl.DeviceIdType.MESH,
        ).start()

    def tell_ids(where):
        pltpu.make_async_remote_copy(
            src_ref=ids_ref.at[me],
            dst_ref=ids_ref.at[me],
            send_sem=ids_send,
            recv_sem=ids_recv,
            device_id=where,
            device_id_type=pl.DeviceIdType.MESH,
        ).start()

    def told_ids(count):
        waiter(ids_ref.at[pl.ds(0, count)], ids_send, ids_recv).wait_send()

    def hear_ids(count):
        waiter(ids_ref.at[pl.ds(0, count)], ids_send, ids_recv).wait_recv()

    def give(at_row, at_col, at_core, best):
        at = spot(at_col * CORES + at_core, at_row)
        given_ref[at] = best
        pltpu.make_async_remote_copy(
            src_ref=given_ref.at[at],
            dst_ref=taken_ref.at[me],
            send_sem=best_send,
            recv_sem=best_recv,
            device_id=device(at_row, at_col, at_core),
            device_id_type=pl.DeviceIdType.MESH,
        ).start()

    def gave(count):
        waiter(given_ref.at[pl.ds(0, count)], best_send, best_recv).wait_send()

    def take(*places):
        with jax.named_scope("w_back"):
            waiter(given_ref.at[pl.ds(0, len(places))], best_send, best_recv).wait_recv()
        best = taken_ref[spot(places[0][0], places[0][1])]
        for at_line, at_row in places[1:]:
            best = jnp.maximum(best, taken_ref[spot(at_line, at_row)])
        return best

    def finish(best):
        out_ref[...] = jnp.where(best > SAME / 2, jnp.maximum(best - SAME, -1.0), -1.0)

    def mark(at_line, at_row):
        shape = (row_count, row_count)
        down = jnp.transpose(jnp.broadcast_to(ids_ref[spot(at_line, at_row)], shape))
        here = down == lax.broadcasted_iota(jnp.int32, shape, 1)
        marks_ref[at_line, at_row] = jnp.where(here, SAME**0.5, 0.0).astype(jnp.bfloat16)

    def flat(ref, *index):
        values = ref[index]
        return values.reshape(-1, values.shape[-1])

    def operand(*indices):
        return jnp.concatenate(
            [
                jnp.concatenate([flat(blocks_ref, *index), flat(marks_ref, *index)], axis=1)
                for index in indices
            ],
            axis=0,
        )

    def scores(left, right):
        return lax.dot_general(
            left, right, (((1,), (1,)), ((), ())), preferred_element_type=jnp.float32
        )

    def down_max(values):
        return jnp.max(values, axis=0, keepdims=True)

    def fold(values):
        folded = values[:, :row_count]
        for at in range(1, values.shape[1] // row_count):
            folded = jnp.maximum(folded, values[:, at * row_count : (at + 1) * row_count])
        return folded

    def turn_max(folded):
        return down_max(jnp.transpose(folded))

    def without_self(values, start):
        down = lax.broadcasted_iota(jnp.int32, values.shape, 0)
        return jnp.where(
            down == lax.broadcasted_iota(jnp.int32, values.shape, 1) + start, -1.0, values
        )

    chip = pl.ds(col * CORES, CORES)

    def split(values):
        low, high = values[:, :row_count], values[:, row_count:]
        return jnp.where(core == 0, low, high), jnp.where(core == 0, high, low)

    def own_best():
        return down_max(
            without_self(scores(operand((chip, row)), operand((line, row))), core * row_count)
        )

    with jax.named_scope('e_small'):
        for copy in small_copies:
            copy.wait()
    counts = jnp.transpose(
        jnp.broadcast_to(lengths_ref[...].astype(jnp.float32), (row_count, row_count))
    )[:, 0:1]
    with jax.named_scope('e_states'):
        states_copy.wait()
    states = states_ref[...]
    summed = states[:, 0, :].astype(jnp.float32)
    for position in range(1, seq_len):
        token = states[:, position, :].astype(jnp.float32)
        summed = summed + jnp.where(counts > position, token, 0.0)
    pooled = (summed / counts).astype(jnp.bfloat16)
    projected = bias_ref[...]
    for at, copy in enumerate(weight_copies):
        with jax.named_scope('e_weight%d' % at):
            copy.wait()
        depth_at = slice(at * slab, (at + 1) * slab)
        projected = projected + jnp.dot(
            pooled[:, depth_at], weight_ref[depth_at], preferred_element_type=jnp.float32
        )
    hidden = jnp.tanh(projected)
    factor = lax.rsqrt(jnp.sum(hidden * hidden, axis=1, keepdims=True) + 1e-06)
    blocks_ref[line, row] = (hidden * factor).astype(jnp.bfloat16)

    with jax.named_scope("w_barrier"):
        pl.semaphore_wait(barrier, greetings)

    each_to(tell_ids)

    flow = jnp.where(row == 0, END, jnp.where(row == 1, NEAR, OUTER))
    for part in range(CHUNKS):
        if part < CHUNKS - ROUND:
            detours = (row == 1) & (core == 1)
        else:
            detours = (row == 1) & around

        @pl.when((row != hub) & jnp.logical_not(detours))
        def _():
            rows = blocks_ref.at[line, row, pl.ds(part * chunk, chunk)]
            pltpu.make_async_remote_copy(
                src_ref=rows,
                dst_ref=rows,
                send_sem=block_send.at[0],
                recv_sem=block_recv.at[flow + part],
                device_id=device(hub, col, core),
                device_id_type=pl.DeviceIdType.MESH,
            ).start()

        @pl.when(detours)
        def _():
            detour_out(part)

    for part in range(CHUNKS):
        send(SIBLING, part, line, row, sibling_device, 4)

    def send_across():
        for part in range(CHUNKS):
            send(ACROSS, part, line, row, device(row, far_col, core), 4)

    later = (row > hub) & (core == 1)

    @pl.when(jnp.logical_not(later))
    def _():
        send_across()

    mark(line, row)

    @pl.when(later)
    def _():
        sent(0, 1)
        send_across()

    @pl.when(row != hub)
    def _():
        for part in range(CHUNKS):
            arrive(ACROSS, part, across_line, row)

            @pl.when(row == 1)
            def _():
                send(AFTER, part, across_line, row, device(0, col, core), 1)

            if part < KEPT:

                @pl.when((row > hub) & (core == 0))
                def _():
                    send(CORNER, part, across_line, row, device(hub, col, core), 1)

        arrived(SIBLING, sibling_line, row)

        @pl.when(row > 0)
        def _():
            hear_ids(2)

        @pl.when(row == 0)
        def _():
            hear_ids(3)

        mark(across_line, row)
        mark(sibling_line, row)
        both = operand((chip, row))
        mine, other = split(down_max(scores(operand((across_line, row)), both)))
        best_ref[0:1] = jnp.maximum(mine, own_best())
        best_ref[1:2] = other

        @pl.when(row == 0)
        def _():
            with jax.named_scope("w_after"):
                arrived(AFTER, across_line, 1)
            mark(across_line, 1)
            after = scores(operand((across_line, 1)), operand((chip, row)))
            give(1, far_col, core, turn_max(fold(after)))
            mine, other = split(down_max(after))
            best_ref[0:1] = jnp.maximum(best_ref[0:1], mine)
            best_ref[1:2] = jnp.maximum(best_ref[1:2], other)

        give(row, col, far_core, best_ref[1:2])
        sent(4, 2)

        @pl.when(jnp.logical_not(later))
        def _():
            sent(0, 1)

        hubs = tuple((col * CORES + at_core, hub) for at_core in range(CORES))

        @pl.when(row == 0)
        def _():
            told_ids(4)
            gave(2)
            finish(jnp.maximum(best_ref[0:1], take((sibling_line, row), *hubs)))

        @pl.when(row == 1)
        def _():
            told_ids(5)
            gave(1)
            sent(1, 1)

            @pl.when(group == 0)
            def _():
                best = take((sibling_line, row), (across_line, 0), *hubs)
                finish(jnp.maximum(best_ref[0:1], best))

            @pl.when(group == 1)
            def _():
                best = take((sibling_line, row), (across_line, 0), (line, hub))
                finish(jnp.maximum(best_ref[0:1], best))

        @pl.when(row > hub)
        def _():
            told_ids(6)
            gave(1)

            @pl.when(core == 0)
            def _():
                sent_parts(1, KEPT)

            @pl.when(group == 0)
            def _():
                best = take((sibling_line, row), (across_line, hub), *hubs)
                finish(jnp.maximum(best_ref[0:1], best))

            @pl.when(group == 1)
            def _():
                far_hub = (far_col * CORES + far_core, hub)
                best = take((sibling_line, row), (across_line, hub), far_hub, *hubs)
                finish(jnp.maximum(best_ref[0:1], best))

    @pl.when(row == hub)
    def _():
        outer, beside, corner = (line, hub + 1), (across_line, hub), (across_line, hub + 1)
        near, end = (line, hub - 1), (line, 0)
        near_too, end_too, outer_too = [(sibling_line, at) for at in (hub - 1, 0, hub + 1)]
        beside_too = (far_col * CORES + far_core, hub)
        corner_too = (far_col * CORES + far_core, hub + 1)
        forward = group == 0
        far_chip = pl.ds(far_col * CORES, CORES)
        width = CORES * row_count

        def detour(part):
            @pl.when(core == 1)
            def _():
                detour_on(part)

        def pass_outer(part):
            arrive(OUTER, part, *outer)
            send(OUTER_TOO, part, *outer, sibling_device, 1)

            @pl.when(True if part >= KEPT else core == 1)
            def _():
                send(CORNER, part, *outer, device(hub, far_col, core), 2)

        def pass_near(part):
            arrive(NEAR, part, *near)

            @pl.when(forward)
            def _():
                send(NEAR_TOO, part, *near, sibling_device, 1)

        def pass_end(part):
            arrive(END, part, *end)
            send(END_TOO, part, *end, sibling_device, 1)

        def pick(values, at):
            low, high = [
                values[:, (2 * at_core + at) * row_count : (2 * at_core + at + 1) * row_count]
                for at_core in range(CORES)
            ]
            return jnp.where(core == 0, low, high), jnp.where(core == 0, high, low)

        @pl.when((core == 0) & passing)
        def _():
            for part in range(CHUNKS - ROUND, CHUNKS):
                detour_on(part)

        with jax.named_scope("w_a"):
            for part in range(2):
                detour(part)
                pass_outer(part)
                pass_end(part)
        with jax.named_scope("w_ids"):
            hear_ids(11)
        for at_row in range(ROWS):
            mark(sibling_line, at_row)
        for place in (outer, near, end, beside, beside_too, corner, corner_too):
            mark(*place)
        with jax.named_scope("w_b"):
            for part in range(2, CHUNKS):
                detour(part)
                pass_outer(part)
                pass_end(part)
        arrived(SIBLING, sibling_line, hub)
        with jax.named_scope("w_beside"):
            for part in range(CHUNKS):
                arrive(ACROSS, part, *beside)
                send(BESIDE_TOO, part, *beside, sibling_device, 1)
        left_size = 2 * row_count
        hubs = operand((chip, hub))
        early = scores(operand((line, hub), outer), hubs)
        early_too = scores(operand(beside, end), hubs)
        own = without_self(early[:row_count], -core * row_count)
        hub_best = jnp.maximum(
            jnp.maximum(down_max(own), down_max(early[row_count:])), down_max(early_too)
        )
        outer_early = turn_max(fold(early[row_count:]))
        early_folded = fold(early_too)
        outers, besides, ends = (chip, hub + 1), (far_chip, hub), (chip, 0)
        with jax.named_scope("w_outer_too"):
            arrived(OUTER_TOO, *outer_too)
        beside_outer = scores(operand(beside), operand(outers))
        end_outer = scores(operand(end), operand(outers))
        outer_low = jnp.maximum(down_max(beside_outer), down_max(end_outer))
        beside_early = turn_max(jnp.maximum(early_folded[:row_count], fold(beside_outer)))
        end_early = turn_max(jnp.maximum(early_folded[row_count:], fold(end_outer)))

        def give_outers(near_outer):
            mine, other = split(jnp.maximum(outer_low, down_max(near_outer)))
            give(hub + 1, col, far_core, other)
            give(hub + 1, col, core, jnp.maximum(outer_early, mine))

        def give_ends(best, folded):
            mine, other = split(best)
            give(0, col, far_core, other)
            mine = jnp.maximum(jnp.maximum(end_early, mine), turn_max(folded))
            give(0, col, core, mine)

        def give_besides(best):
            mine, other = split(best)
            give(hub, far_col, far_core, other)
            give(hub, far_col, core, jnp.maximum(beside_early, mine))

        def give_hubs(hub_scores):
            mine, other = split(jnp.maximum(hub_best, down_max(hub_scores)))
            give(hub, col, far_core, other)
            best_ref[0:1] = mine

        @pl.when(group == 0)
        def _():
            with jax.named_scope("w_near"):
                for part in range(CHUNKS):
                    pass_near(part)
            with jax.named_scope("w_too"):
                arrived(BESIDE_TOO, *beside_too)
                arrived(END_TOO, *end_too)
            end_beside = scores(operand(end), operand(besides))
            near_end = scores(operand(near), operand(ends))
            with jax.named_scope("w_corner"):
                arrived(CORNER, *corner)
            corner_operand = operand(corner)
            corner_end = jnp.concatenate(
                [
                    scores(corner_operand, operand((col * CORES + at_core, 0)))
                    for at_core in range(CORES)
                ],
                axis=1,
            )
            give_ends(
                jnp.maximum(down_max(near_end), down_max(corner_end)), fold(end_beside)
            )
            near_outer = scores(operand(near), operand(outers))
            near_beside = scores(operand(near), operand(besides))
            give_outers(near_outer)
            near_folded = jnp.maximum(
                fold(near_end), jnp.maximum(fold(near_outer), fold(near_beside))
            )
            with jax.named_scope("w_near_too"):
                arrived(NEAR_TOO, *near_too)
            corner_near = scores(operand(corner), operand((chip, hub - 1)))
            hub_scores = scores(operand(near), hubs)
            give(
                hub + 1, far_col, core, turn_max(jnp.maximum(fold(corner_end), fold(corner_near)))
            )
            mine, other = split(down_max(corner_near))
            give(hub - 1, col, far_core, other)
            near_best = turn_max(jnp.maximum(near_folded, fold(hub_scores)))
            give(hub - 1, col, core, jnp.maximum(near_best, mine))
            give_besides(jnp.maximum(down_max(end_beside), down_max(near_beside)))
            give_hubs(hub_scores)

        @pl.when(group == 1)
        def _():
            with jax.named_scope("w_corner"):
                arrived(CORNER, *corner)
            for part in range(CHUNKS):
                send(CORNER_TOO, part, *corner, sibling_device, 1)
            for part in range(CHUNKS):
                with jax.named_scope("w_near%d" % part):
                    pass_near(part)
            with jax.named_scope("w_too"):
                arrived(BESIDE_TOO, *beside_too)
                arrived(END_TOO, *end_too)
                arrived(CORNER_TOO, *corner_too)
            left = operand(end, near)
            near_outer = scores(operand(near), operand(outers))
            left_corner = scores(left, operand((far_chip, hub + 1)))
            give_outers(near_outer)
            mine, other = split(down_max(left_corner))
            give(hub + 1, far_col, far_core, other)
            give(hub + 1, far_col, core, mine)
            left_beside = scores(left, operand(besides))
            near_end = scores(operand(near), operand(ends))
            left_folded = jnp.maximum(fold(left_corner), fold(left_beside))
            give_ends(down_max(near_end), left_folded[:row_count])
            hub_scores = scores(operand(near), hubs)
            near_folded = jnp.maximum(
                jnp.maximum(fold(near_end), fold(near_outer)),
                jnp.maximum(left_folded[row_count:], fold(hub_scores)),
            )
            give(hub - 1, col, core, turn_max(near_folded))
            give_besides(down_max(left_beside))
            give_hubs(hub_scores)

        sent(4, 2)
        sent(1, 4)

        @pl.when(core == 1)
        def _():
            sent(2, 1)
            sent(3, 1)

        @pl.when(core == 0)
        def _():
            pass

        @pl.when((core == 0) & passing)
        def _():
            sent_parts(3, ROUND)

        told_ids(3)
        gave(10)
        finish(jnp.maximum(best_ref[0:1], take((sibling_line, hub), (across_line, hub), beside_too)))


def meet_body(token_states, lengths, cluster_id, proj_weight, proj_bias):
    row_count, seq_len, feat_dim = token_states.shape
    lines = lax.axis_size("docs") // ROWS * CORES
    vmem = pl.BlockSpec(memory_space=pltpu.VMEM)
    hbm = pl.BlockSpec(memory_space=pl.ANY)
    result = pl.pallas_call(
        meet_kernel,
        out_shape=pltpu.VMEM((1, row_count), jnp.float32),
        in_specs=[hbm] * 5,
        out_specs=vmem,
        scratch_shapes=[
            pltpu.VMEM((1, row_count), jnp.int32),
            pltpu.VMEM((1, feat_dim), jnp.float32),
            pltpu.VMEM(token_states.shape, jnp.bfloat16),
            pltpu.VMEM(proj_weight.shape, jnp.bfloat16),
            pltpu.VMEM((lines * ROWS, 1, row_count), jnp.int32),
            pltpu.VMEM((lines, ROWS, row_count, feat_dim), jnp.bfloat16),
            pltpu.VMEM((lines, ROWS, row_count, row_count), jnp.bfloat16),
            pltpu.VMEM((row_count, feat_dim), jnp.bfloat16),
            pltpu.VMEM((2, row_count), jnp.float32),
            pltpu.VMEM((lines * ROWS, 1, row_count), jnp.float32),
            pltpu.VMEM((lines * ROWS, 1, row_count), jnp.float32),
            pltpu.SemaphoreType.DMA((5,)),
            pltpu.SemaphoreType.DMA((FLOWS,)),
            pltpu.SemaphoreType.DMA((CHUNKS,)),
            pltpu.SemaphoreType.DMA,
            pltpu.SemaphoreType.DMA,
            pltpu.SemaphoreType.DMA,
            pltpu.SemaphoreType.DMA,
        ],
        compiler_params=pltpu.CompilerParams(collective_id=0, has_side_effects=True),
        name="scores",
    )(token_states, lengths[None, :], cluster_id[None, :], proj_weight, proj_bias[None, :])
    return result.reshape(row_count)

def solution(mesh):
    in_specs = (
        P(("groups", "docs", "help"), None, None),
        P(("groups", "docs", "help")),
        P(("groups", "docs", "help")),
        P(),
        P(),
    )
    out_specs = P(("groups", "docs", "help"))
    meets = mesh.shape["docs"] == 2 * ROWS and mesh.shape["help"] == CORES and mesh.shape["groups"] == 2
    return jax.shard_map(meet_body if meets else body, mesh=mesh, in_specs=in_specs, out_specs=out_specs, check_vma=False)
```

```python
import jax
import jax.numpy as jnp
from jax import lax
from jax.experimental import pallas as pl
from jax.experimental.pallas import tpu as pltpu
from jax.sharding import PartitionSpec as P

CL_OWN = 1


def partner(value, axis, bit):
    return lax.ppermute(value, axis, [(i, i ^ 1 << bit) for i in range(lax.axis_size(axis))])


def slot_maxima(own_emb, own_ids, self_pos, col_emb, col_ids):
    row_total = own_emb.shape[0]
    block = min(row_total, 512)
    col_pos = lax.broadcasted_iota(jnp.int32, (col_emb.shape[0],), 0)

    def block_max(pieces):
        part_emb, part_ids, part_self = pieces
        duplicate_scores = jnp.einsum(
            "rd,cd->rc", part_emb, col_emb, preferred_element_type=jnp.float32
        )
        match = (
            (part_ids[:, None] == col_ids[None, :])
            & (col_ids[None, :] >= 0)
            & (part_self[:, None] != col_pos[None, :])
        )
        return jnp.max(jnp.where(match, duplicate_scores, -1.0), axis=1)

    steps_count = row_total // block
    result = lax.map(
        block_max,
        (
            own_emb.reshape(steps_count, block, own_emb.shape[1]),
            own_ids.reshape(steps_count, block),
            self_pos.reshape(steps_count, block),
        ),
    )
    return result.reshape(row_total)


def body(token_states, lengths, cluster_id, proj_weight, proj_bias):
    row_count, seq_len, feat_dim = token_states.shape
    owners = lax.axis_size("docs")
    slot_cap = 2 * row_count // owners
    position_count = owners * slot_cap
    token_mask = (
        lax.broadcasted_iota(jnp.int32, (row_count, seq_len), 1) < lengths[:, None]
    ).astype(jnp.bfloat16)
    summed = jnp.einsum("rsd,rs->rd", token_states, token_mask, preferred_element_type=jnp.float32)
    pooled = (summed / lengths[:, None].astype(jnp.float32)).astype(jnp.bfloat16)
    hidden = jnp.tanh(jnp.dot(pooled, proj_weight, preferred_element_type=jnp.float32) + proj_bias)
    factor = lax.rsqrt(jnp.sum(hidden * hidden, axis=1, keepdims=True) + 1e-06)
    embedded = (hidden * factor).astype(jnp.bfloat16)
    dest_owner = cluster_id // CL_OWN
    same_owner = dest_owner[:, None] == dest_owner[None, :]
    earlier = lax.broadcasted_iota(jnp.int32, (row_count, row_count), 1) < lax.broadcasted_iota(
        jnp.int32, (row_count, row_count), 0
    )
    slot_rank = jnp.sum((same_owner & earlier).astype(jnp.int32), axis=1)
    target = dest_owner * slot_cap + slot_rank
    chooser = lax.broadcasted_iota(jnp.int32, (position_count, row_count), 0) == target[None, :]
    packed = jnp.dot(
        chooser.astype(jnp.bfloat16), embedded, preferred_element_type=jnp.float32
    ).astype(jnp.bfloat16)
    packed_ids = jnp.max(jnp.where(chooser, cluster_id[None, :], -1), axis=1)
    own_emb, own_ids = (
        lax.all_to_all(packed, "docs", split_axis=0, concat_axis=0, tiled=True),
        lax.all_to_all(packed_ids, "docs", split_axis=0, concat_axis=0, tiled=True),
    )
    mate_emb, mate_ids = partner((own_emb, own_ids), "help", 0)
    col_emb = jnp.concatenate([own_emb, mate_emb], axis=0)
    col_ids = jnp.concatenate([own_ids, mate_ids], axis=0)
    self_pos = lax.broadcasted_iota(jnp.int32, (position_count,), 0)
    maxima = slot_maxima(own_emb, own_ids, self_pos, col_emb, col_ids)
    returned = lax.all_to_all(maxima, "docs", split_axis=0, concat_axis=0, tiled=True)
    return jnp.max(jnp.where(chooser, returned[:, None], -3.0), axis=0)


ROWS = 4
CORES = 2
CHUNKS = 4
SLABS = 2
ROUND = 1
SAME = 4.0
SIBLING, CORNER, NEAR_TOO, END_TOO, OUTER_TOO, BESIDE_TOO = range(6)
AFTER, CORNER_TOO, WHOLE = CORNER, NEAR_TOO, BESIDE_TOO
ACROSS, OUTER, NEAR, END = (WHOLE + 1 + CHUNKS * at for at in range(4))
FLOWS = END + CHUNKS


def meet_kernel(
    states_hbm,
    lengths_hbm,
    ids_hbm,
    weight_hbm,
    bias_hbm,
    out_ref,
    lengths_ref,
    bias_ref,
    states_ref,
    weight_ref,
    ids_ref,
    blocks_ref,
    marks_ref,
    detour_ref,
    best_ref,
    given_ref,
    taken_ref,
    block_send,
    block_recv,
    detour_recv,
    ids_send,
    ids_recv,
    best_send,
    best_recv,
):
    row_count, seq_len, feat_dim = states_ref.shape
    lines = blocks_ref.shape[0]
    columns = lines // CORES
    chunk = row_count // CHUNKS
    hub = ROWS - 2
    group = lax.axis_index("groups")
    docs = lax.axis_index("docs")
    core = lax.axis_index("help")
    depth = docs // columns
    col = docs % columns
    row = depth + group * (ROWS - 1 - 2 * depth)
    far_col = columns - 1 - col
    far_core = CORES - 1 - core
    line = col * CORES + core
    sibling_line = col * CORES + far_core
    across_line = far_col * CORES + core

    def device(at_row, at_col, at_core):
        at_depth = at_row + group * (ROWS - 1 - 2 * at_row)
        return {"docs": at_depth * columns + at_col, "help": at_core}

    def other_plane(at_row):
        at_depth = at_row + group * (ROWS - 1 - 2 * at_row)
        return {"groups": 1 - group, "docs": at_depth * columns + col, "help": core}

    def spot(at_line, at_row):
        return at_line * ROWS + at_row

    me = spot(line, row)
    sibling_device = device(row, col, far_core)

    states_copy = pltpu.make_async_copy(states_hbm, states_ref, block_send.at[3])
    states_copy.start()
    small_copies = [
        pltpu.make_async_copy(source, held, block_send.at[position])
        for position, (source, held) in enumerate(
            [(lengths_hbm, lengths_ref), (ids_hbm, ids_ref.at[me]), (bias_hbm, bias_ref)]
        )
    ]
    for copy in small_copies:
        copy.start()
    slab = feat_dim // SLABS
    weight_copies = [
        pltpu.make_async_copy(
            weight_hbm.at[pl.ds(at * slab, slab)],
            weight_ref.at[pl.ds(at * slab, slab)],
            best_send if at else block_send.at[4],
        )
        for at in range(SLABS)
    ]

    barrier = pltpu.get_barrier_semaphore()

    def greet(*wheres):
        for where in wheres:
            pl.semaphore_signal(
                barrier, inc=1, device_id=where, device_id_type=pl.DeviceIdType.MESH
            )

    around = (core == 1) | (group == 1)
    passing = (core == 1) | (group == 0)

    def each_to(act):
        @pl.when(row != hub)
        def _():
            for at_core in range(CORES):
                act(device(hub, col, at_core))

        @pl.when(row == 1)
        def _():
            act(device(0, far_col, core))

        @pl.when(row == hub)
        def _():
            act(device(hub, far_col, far_core))

        @pl.when(row > hub)
        def _():
            for at_core in range(CORES):
                act(device(hub, far_col, at_core))

        act(device(row, far_col, core))
        act(sibling_device)

    each_to(lambda where: greet(where))

    @pl.when(row == 0)
    def _():
        greet(device(1, col, core), device(1, far_col, core))

    @pl.when(row == 1)
    def _():
        greet(device(0, col, core))

    @pl.when(row == hub)
    def _():
        for at_core in range(CORES):
            for at_row in (0, 1, hub + 1):
                greet(device(at_row, col, at_core))
            greet(device(hub + 1, far_col, at_core))

    @pl.when((row == 1) & around)
    def _():
        greet(other_plane(row))

    @pl.when((row == hub) & passing)
    def _():
        greet(other_plane(row), other_plane(hub - 1))

    @pl.when((row == hub) & around & jnp.logical_not((core == 1) & passing))
    def _():
        greet(other_plane(hub - 1))

    for copy in weight_copies:
        copy.start()

    greetings = (
        2
        + 4 * (row < hub)
        + 9 * (row == hub)
        + 4 * (row > hub)
        + ((row == 1) & around)
        + (row == hub) * (1 + passing)
    )

    def send(flow, part, at_line, at_row, where, lane=0):
        rows = blocks_ref.at[at_line, at_row, pl.ds(part * chunk, chunk)]
        pltpu.make_async_remote_copy(
            src_ref=rows,
            dst_ref=rows,
            send_sem=block_send.at[lane],
            recv_sem=block_recv.at[flow if flow <= WHOLE else flow + part],
            device_id=where,
            device_id_type=pl.DeviceIdType.MESH,
        ).start()

    def waiter(held, send_sem, recv_sem):
        return pltpu.make_async_remote_copy(
            src_ref=held,
            dst_ref=held,
            send_sem=send_sem,
            recv_sem=recv_sem,
            device_id=sibling_device,
            device_id_type=pl.DeviceIdType.MESH,
        )

    def sent(lane, count):
        waiter(
            blocks_ref.at[0, pl.ds(0, count)], block_send.at[lane], block_recv.at[0]
        ).wait_send()

    def sent_parts(lane, count):
        rows = blocks_ref.at[0, 0, pl.ds(0, count * chunk)]
        waiter(rows, block_send.at[lane], block_recv.at[0]).wait_send()

    def arrive(flow, part, at_line, at_row):
        rows = blocks_ref.at[at_line, at_row, pl.ds(part * chunk, chunk)]
        waiter(rows, block_send.at[0], block_recv.at[flow + part]).wait_recv()

    def arrived(flow, at_line, at_row):
        waiter(
            blocks_ref.at[at_line, at_row], block_send.at[0], block_recv.at[flow]
        ).wait_recv()

    def detour_out(part):
        rows = pl.ds(part * chunk, chunk)
        pltpu.make_async_remote_copy(
            src_ref=blocks_ref.at[line, row, rows],
            dst_ref=detour_ref.at[rows],
            send_sem=block_send.at[0],
            recv_sem=detour_recv.at[part],
            device_id=other_plane(row),
            device_id_type=pl.DeviceIdType.MESH,
        ).start()

    def detour_on(part):
        rows = pl.ds(part * chunk, chunk)
        waiter(detour_ref.at[rows], block_send.at[0], detour_recv.at[part]).wait_recv()
        pltpu.make_async_remote_copy(
            src_ref=detour_ref.at[rows],
            dst_ref=blocks_ref.at[line, hub - 1, rows],
            send_sem=block_send.at[3],
            recv_sem=block_recv.at[NEAR + part],
            device_id=other_plane(hub - 1),
            device_id_type=pl.DeviceIdType.MESH,
        ).start()

    def tell_ids(where):
        pltpu.make_async_remote_copy(
            src_ref=ids_ref.at[me],
            dst_ref=ids_ref.at[me],
            send_sem=ids_send,
            recv_sem=ids_recv,
            device_id=where,
            device_id_type=pl.DeviceIdType.MESH,
        ).start()

    def told_ids(count):
        waiter(ids_ref.at[pl.ds(0, count)], ids_send, ids_recv).wait_send()

    def hear_ids(count):
        waiter(ids_ref.at[pl.ds(0, count)], ids_send, ids_recv).wait_recv()

    def give(at_row, at_col, at_core, best):
        at = spot(at_col * CORES + at_core, at_row)
        given_ref[at] = best
        pltpu.make_async_remote_copy(
            src_ref=given_ref.at[at],
            dst_ref=taken_ref.at[me],
            send_sem=best_send,
            recv_sem=best_recv,
            device_id=device(at_row, at_col, at_core),
            device_id_type=pl.DeviceIdType.MESH,
        ).start()

    def gave(count):
        waiter(given_ref.at[pl.ds(0, count)], best_send, best_recv).wait_send()

    def take(*places):
        with jax.named_scope("w_back"):
            waiter(given_ref.at[pl.ds(0, len(places))], best_send, best_recv).wait_recv()
        best = taken_ref[spot(places[0][0], places[0][1])]
        for at_line, at_row in places[1:]:
            best = jnp.maximum(best, taken_ref[spot(at_line, at_row)])
        return best

    def finish(best):
        out_ref[...] = jnp.where(best > SAME / 2, jnp.maximum(best - SAME, -1.0), -1.0)

    def mark(at_line, at_row):
        shape = (row_count, row_count)
        down = jnp.transpose(jnp.broadcast_to(ids_ref[spot(at_line, at_row)], shape))
        here = down == lax.broadcasted_iota(jnp.int32, shape, 1)
        marks_ref[at_line, at_row] = jnp.where(here, SAME**0.5, 0.0).astype(jnp.bfloat16)

    def flat(ref, *index):
        values = ref[index]
        return values.reshape(-1, values.shape[-1])

    def operand(*indices):
        return jnp.concatenate(
            [
                jnp.concatenate([flat(blocks_ref, *index), flat(marks_ref, *index)], axis=1)
                for index in indices
            ],
            axis=0,
        )

    def scores(left, right):
        return lax.dot_general(
            left, right, (((1,), (1,)), ((), ())), preferred_element_type=jnp.float32
        )

    def down_max(values):
        return jnp.max(values, axis=0, keepdims=True)

    def fold(values):
        folded = values[:, :row_count]
        for at in range(1, values.shape[1] // row_count):
            folded = jnp.maximum(folded, values[:, at * row_count : (at + 1) * row_count])
        return folded

    def turn_max(folded):
        return down_max(jnp.transpose(folded))

    def without_self(values, start):
        down = lax.broadcasted_iota(jnp.int32, values.shape, 0)
        return jnp.where(
            down == lax.broadcasted_iota(jnp.int32, values.shape, 1) + start, -1.0, values
        )

    chip = pl.ds(col * CORES, CORES)

    def split(values):
        low, high = values[:, :row_count], values[:, row_count:]
        return jnp.where(core == 0, low, high), jnp.where(core == 0, high, low)

    def own_best():
        return down_max(
            without_self(scores(operand((chip, row)), operand((line, row))), core * row_count)
        )

    with jax.named_scope('e_small'):
        for copy in small_copies:
            copy.wait()
    counts = jnp.transpose(
        jnp.broadcast_to(lengths_ref[...].astype(jnp.float32), (row_count, row_count))
    )[:, 0:1]
    with jax.named_scope('e_states'):
        states_copy.wait()
    states = states_ref[...]
    summed = states[:, 0, :].astype(jnp.float32)
    for position in range(1, seq_len):
        token = states[:, position, :].astype(jnp.float32)
        summed = summed + jnp.where(counts > position, token, 0.0)
    pooled = (summed / counts).astype(jnp.bfloat16)
    projected = bias_ref[...]
    for at, copy in enumerate(weight_copies):
        with jax.named_scope('e_weight%d' % at):
            copy.wait()
        depth_at = slice(at * slab, (at + 1) * slab)
        projected = projected + jnp.dot(
            pooled[:, depth_at], weight_ref[depth_at], preferred_element_type=jnp.float32
        )
    hidden = jnp.tanh(projected)
    factor = lax.rsqrt(jnp.sum(hidden * hidden, axis=1, keepdims=True) + 1e-06)
    blocks_ref[line, row] = (hidden * factor).astype(jnp.bfloat16)

    with jax.named_scope("w_barrier"):
        pl.semaphore_wait(barrier, greetings)

    each_to(tell_ids)

    flow = jnp.where(row == 0, END, jnp.where(row == 1, NEAR, OUTER))
    for part in range(CHUNKS):
        if part < CHUNKS - ROUND:
            detours = (row == 1) & (core == 1)
        else:
            detours = (row == 1) & around

        @pl.when((row != hub) & jnp.logical_not(detours))
        def _():
            rows = blocks_ref.at[line, row, pl.ds(part * chunk, chunk)]
            pltpu.make_async_remote_copy(
                src_ref=rows,
                dst_ref=rows,
                send_sem=block_send.at[0],
                recv_sem=block_recv.at[flow + part],
                device_id=device(hub, col, core),
                device_id_type=pl.DeviceIdType.MESH,
            ).start()

        @pl.when(detours)
        def _():
            detour_out(part)

    for part in range(CHUNKS):
        send(SIBLING, part, line, row, sibling_device, 4)

    def send_across(*parts):
        for part in parts:
            send(ACROSS, part, line, row, device(row, far_col, core), 4)

    later = (row > hub) & (core == 1)

    @pl.when(jnp.logical_not(later))
    def _():
        send_across(*range(CHUNKS))

    @pl.when(later)
    def _():
        send_across(CHUNKS - 1)

    mark(line, row)

    @pl.when(later)
    def _():
        sent(0, 1)
        send_across(*range(CHUNKS - 1))

    @pl.when(row != hub)
    def _():
        @pl.when(row < hub)
        def _():
            for part in range(CHUNKS):
                arrive(ACROSS, part, across_line, row)

                @pl.when(row == 1)
                def _():
                    send(AFTER, part, across_line, row, device(0, col, core), 1)

        @pl.when(row > hub)
        def _():
            @pl.when(core == 0)
            def _():
                for part in range(CHUNKS):
                    arrive(ACROSS, part, across_line, row)
                    if part:
                        send(CORNER, part, across_line, row, device(hub, col, core), 1)

            @pl.when(core == 1)
            def _():
                for part in (CHUNKS - 1, *range(CHUNKS - 1)):
                    arrive(ACROSS, part, across_line, row)
                    if part == CHUNKS - 1:
                        send(CORNER, part, across_line, row, device(hub, col, core), 1)

        arrived(SIBLING, sibling_line, row)

        @pl.when(row > 0)
        def _():
            hear_ids(2)

        @pl.when(row == 0)
        def _():
            hear_ids(3)

        mark(across_line, row)
        mark(sibling_line, row)
        both = operand((chip, row))
        mine, other = split(down_max(scores(operand((across_line, row)), both)))
        best_ref[0:1] = jnp.maximum(mine, own_best())
        best_ref[1:2] = other

        @pl.when(row == 0)
        def _():
            with jax.named_scope("w_after"):
                arrived(AFTER, across_line, 1)
            mark(across_line, 1)
            after = scores(operand((across_line, 1)), operand((chip, row)))
            give(1, far_col, core, turn_max(fold(after)))
            mine, other = split(down_max(after))
            best_ref[0:1] = jnp.maximum(best_ref[0:1], mine)
            best_ref[1:2] = jnp.maximum(best_ref[1:2], other)

        give(row, col, far_core, best_ref[1:2])
        sent(4, 2)

        @pl.when(jnp.logical_not(later))
        def _():
            sent(0, 1)

        hubs = tuple((col * CORES + at_core, hub) for at_core in range(CORES))

        @pl.when(row == 0)
        def _():
            told_ids(4)
            gave(2)
            finish(jnp.maximum(best_ref[0:1], take((sibling_line, row), *hubs)))

        @pl.when(row == 1)
        def _():
            told_ids(5)
            gave(1)
            sent(1, 1)

            @pl.when(group == 0)
            def _():
                best = take((sibling_line, row), (across_line, 0), *hubs)
                finish(jnp.maximum(best_ref[0:1], best))

            @pl.when(group == 1)
            def _():
                best = take((sibling_line, row), (across_line, 0), (line, hub))
                finish(jnp.maximum(best_ref[0:1], best))

        @pl.when(row > hub)
        def _():
            told_ids(6)
            gave(1)

            @pl.when(core == 0)
            def _():
                sent_parts(1, CHUNKS - 1)

            @pl.when(core == 1)
            def _():
                sent_parts(1, 1)

            @pl.when(group == 0)
            def _():
                best = take((sibling_line, row), (across_line, hub), *hubs)
                finish(jnp.maximum(best_ref[0:1], best))

            @pl.when(group == 1)
            def _():
                far_hub = (far_col * CORES + far_core, hub)
                best = take((sibling_line, row), (across_line, hub), far_hub, *hubs)
                finish(jnp.maximum(best_ref[0:1], best))

    @pl.when(row == hub)
    def _():
        outer, beside, corner = (line, hub + 1), (across_line, hub), (across_line, hub + 1)
        near, end = (line, hub - 1), (line, 0)
        near_too, end_too, outer_too = [(sibling_line, at) for at in (hub - 1, 0, hub + 1)]
        beside_too = (far_col * CORES + far_core, hub)
        corner_too = (far_col * CORES + far_core, hub + 1)
        forward = group == 0
        far_chip = pl.ds(far_col * CORES, CORES)
        width = CORES * row_count

        def detour(part):
            @pl.when(core == 1)
            def _():
                detour_on(part)

        def pass_outer(part):
            arrive(OUTER, part, *outer)
            send(OUTER_TOO, part, *outer, sibling_device, 1)

            if part < CHUNKS - 1:

                @pl.when(core == 1 if part else core >= 0)
                def _():
                    send(CORNER, part, *outer, device(hub, far_col, core), 2)

        def pass_near(part):
            arrive(NEAR, part, *near)

            @pl.when(forward)
            def _():
                send(NEAR_TOO, part, *near, sibling_device, 1)

        def pass_end(part):
            arrive(END, part, *end)
            send(END_TOO, part, *end, sibling_device, 1)

        def pick(values, at):
            low, high = [
                values[:, (2 * at_core + at) * row_count : (2 * at_core + at + 1) * row_count]
                for at_core in range(CORES)
            ]
            return jnp.where(core == 0, low, high), jnp.where(core == 0, high, low)

        @pl.when((core == 0) & passing)
        def _():
            for part in range(CHUNKS - ROUND, CHUNKS):
                detour_on(part)

        with jax.named_scope("w_a"):
            for part in range(2):
                detour(part)
                pass_outer(part)
                pass_end(part)
        with jax.named_scope("w_ids"):
            hear_ids(11)
        for at_row in range(ROWS):
            mark(sibling_line, at_row)
        for place in (outer, near, end, beside, beside_too, corner, corner_too):
            mark(*place)
        with jax.named_scope("w_b"):
            for part in range(2, CHUNKS):
                detour(part)
                pass_outer(part)
                pass_end(part)
        arrived(SIBLING, sibling_line, hub)
        with jax.named_scope("w_beside"):
            for part in range(CHUNKS):
                arrive(ACROSS, part, *beside)
                send(BESIDE_TOO, part, *beside, sibling_device, 1)
        left_size = 2 * row_count
        hubs = operand((chip, hub))
        early = scores(operand((line, hub), outer), hubs)
        early_too = scores(operand(beside, end), hubs)
        own = without_self(early[:row_count], -core * row_count)
        hub_best = jnp.maximum(
            jnp.maximum(down_max(own), down_max(early[row_count:])), down_max(early_too)
        )
        outer_early = turn_max(fold(early[row_count:]))
        early_folded = fold(early_too)
        outers, besides, ends = (chip, hub + 1), (far_chip, hub), (chip, 0)
        with jax.named_scope("w_outer_too"):
            arrived(OUTER_TOO, *outer_too)
        beside_outer = scores(operand(beside), operand(outers))
        end_outer = scores(operand(end), operand(outers))
        outer_low = jnp.maximum(down_max(beside_outer), down_max(end_outer))
        beside_early = turn_max(jnp.maximum(early_folded[:row_count], fold(beside_outer)))
        end_early = turn_max(jnp.maximum(early_folded[row_count:], fold(end_outer)))

        def give_outers(near_outer):
            mine, other = split(jnp.maximum(outer_low, down_max(near_outer)))
            give(hub + 1, col, far_core, other)
            give(hub + 1, col, core, jnp.maximum(outer_early, mine))

        def give_ends(best, folded):
            mine, other = split(best)
            give(0, col, far_core, other)
            mine = jnp.maximum(jnp.maximum(end_early, mine), turn_max(folded))
            give(0, col, core, mine)

        def give_besides(best):
            mine, other = split(best)
            give(hub, far_col, far_core, other)
            give(hub, far_col, core, jnp.maximum(beside_early, mine))

        def give_hubs(hub_scores):
            mine, other = split(jnp.maximum(hub_best, down_max(hub_scores)))
            give(hub, col, far_core, other)
            best_ref[0:1] = mine

        @pl.when(group == 0)
        def _():
            with jax.named_scope("w_near"):
                for part in range(CHUNKS):
                    pass_near(part)
            with jax.named_scope("w_too"):
                arrived(BESIDE_TOO, *beside_too)
                arrived(END_TOO, *end_too)
            end_beside = scores(operand(end), operand(besides))
            near_end = scores(operand(near), operand(ends))
            with jax.named_scope("w_corner"):
                arrived(CORNER, *corner)
            corner_operand = operand(corner)
            corner_end = jnp.concatenate(
                [
                    scores(corner_operand, operand((col * CORES + at_core, 0)))
                    for at_core in range(CORES)
                ],
                axis=1,
            )
            give_ends(
                jnp.maximum(down_max(near_end), down_max(corner_end)), fold(end_beside)
            )
            near_outer = scores(operand(near), operand(outers))
            near_beside = scores(operand(near), operand(besides))
            give_outers(near_outer)
            near_folded = jnp.maximum(
                fold(near_end), jnp.maximum(fold(near_outer), fold(near_beside))
            )
            with jax.named_scope("w_near_too"):
                arrived(NEAR_TOO, *near_too)
            corner_near = scores(operand(corner), operand((chip, hub - 1)))
            hub_scores = scores(operand(near), hubs)
            give(
                hub + 1, far_col, core, turn_max(jnp.maximum(fold(corner_end), fold(corner_near)))
            )
            mine, other = split(down_max(corner_near))
            give(hub - 1, col, far_core, other)
            near_best = turn_max(jnp.maximum(near_folded, fold(hub_scores)))
            give(hub - 1, col, core, jnp.maximum(near_best, mine))
            give_besides(jnp.maximum(down_max(end_beside), down_max(near_beside)))
            give_hubs(hub_scores)

        @pl.when(group == 1)
        def _():
            with jax.named_scope("w_corner"):
                arrived(CORNER, *corner)
            for part in range(CHUNKS):
                send(CORNER_TOO, part, *corner, sibling_device, 1)
            for part in range(CHUNKS):
                with jax.named_scope("w_near%d" % part):
                    pass_near(part)
            with jax.named_scope("w_too"):
                arrived(BESIDE_TOO, *beside_too)
                arrived(END_TOO, *end_too)
                arrived(CORNER_TOO, *corner_too)
            left = operand(end, near)
            near_outer = scores(operand(near), operand(outers))
            left_corner = scores(left, operand((far_chip, hub + 1)))
            give_outers(near_outer)
            mine, other = split(down_max(left_corner))
            give(hub + 1, far_col, far_core, other)
            give(hub + 1, far_col, core, mine)
            left_beside = scores(left, operand(besides))
            near_end = scores(operand(near), operand(ends))
            left_folded = jnp.maximum(fold(left_corner), fold(left_beside))
            give_ends(down_max(near_end), left_folded[:row_count])
            hub_scores = scores(operand(near), hubs)
            near_folded = jnp.maximum(
                jnp.maximum(fold(near_end), fold(near_outer)),
                jnp.maximum(left_folded[row_count:], fold(hub_scores)),
            )
            give(hub - 1, col, core, turn_max(near_folded))
            give_besides(down_max(left_beside))
            give_hubs(hub_scores)

        sent(4, 2)
        sent(1, 4)

        @pl.when(core == 1)
        def _():
            sent_parts(2, CHUNKS - 1)
            sent(3, 1)

        @pl.when(core == 0)
        def _():
            sent_parts(2, 1)

        @pl.when((core == 0) & passing)
        def _():
            sent_parts(3, ROUND)

        told_ids(3)
        gave(10)
        finish(jnp.maximum(best_ref[0:1], take((sibling_line, hub), (across_line, hub), beside_too)))


def meet_body(token_states, lengths, cluster_id, proj_weight, proj_bias):
    row_count, seq_len, feat_dim = token_states.shape
    lines = lax.axis_size("docs") // ROWS * CORES
    vmem = pl.BlockSpec(memory_space=pltpu.VMEM)
    hbm = pl.BlockSpec(memory_space=pl.ANY)
    result = pl.pallas_call(
        meet_kernel,
        out_shape=pltpu.VMEM((1, row_count), jnp.float32),
        in_specs=[hbm] * 5,
        out_specs=vmem,
        scratch_shapes=[
            pltpu.VMEM((1, row_count), jnp.int32),
            pltpu.VMEM((1, feat_dim), jnp.float32),
            pltpu.VMEM(token_states.shape, jnp.bfloat16),
            pltpu.VMEM(proj_weight.shape, jnp.bfloat16),
            pltpu.VMEM((lines * ROWS, 1, row_count), jnp.int32),
            pltpu.VMEM((lines, ROWS, row_count, feat_dim), jnp.bfloat16),
            pltpu.VMEM((lines, ROWS, row_count, row_count), jnp.bfloat16),
            pltpu.VMEM((row_count, feat_dim), jnp.bfloat16),
            pltpu.VMEM((2, row_count), jnp.float32),
            pltpu.VMEM((lines * ROWS, 1, row_count), jnp.float32),
            pltpu.VMEM((lines * ROWS, 1, row_count), jnp.float32),
            pltpu.SemaphoreType.DMA((5,)),
            pltpu.SemaphoreType.DMA((FLOWS,)),
            pltpu.SemaphoreType.DMA((CHUNKS,)),
            pltpu.SemaphoreType.DMA,
            pltpu.SemaphoreType.DMA,
            pltpu.SemaphoreType.DMA,
            pltpu.SemaphoreType.DMA,
        ],
        compiler_params=pltpu.CompilerParams(collective_id=0, has_side_effects=True),
        name="scores",
    )(token_states, lengths[None, :], cluster_id[None, :], proj_weight, proj_bias[None, :])
    return result.reshape(row_count)

def solution(mesh):
    in_specs = (
        P(("groups", "docs", "help"), None, None),
        P(("groups", "docs", "help")),
        P(("groups", "docs", "help")),
        P(),
        P(),
    )
    out_specs = P(("groups", "docs", "help"))
    meets = mesh.shape["docs"] == 2 * ROWS and mesh.shape["help"] == CORES and mesh.shape["groups"] == 2
    return jax.shard_map(meet_body if meets else body, mesh=mesh, in_specs=in_specs, out_specs=out_specs, check_vma=False)
```
